256 devices in a mesh: dp: 2 (over core), ctx: 32 (over y, z), head: 4 (over x).
Axes of the slice: x: 4, y: 4, z: 8, core: 2. Of those that a mesh axis runs over, the one named last changes fastest.
Arguments:
- queries: bfloat16 [2, 8192, 1024], P('dp', 'ctx', 'head'), may hold values from -0.59765625 to 0.59765625
- key_vectors: bfloat16 [2, 8192, 1024], P('dp', 'ctx', 'head'), may hold values from -0.59765625 to 0.59765625
- value_vectors: bfloat16 [2, 8192, 1024], P('dp', 'ctx', 'head'), may hold values from -0.59765625 to 0.59765625
- out_cotangent: bfloat16 [2, 8192, 1024], P('dp', 'ctx'), may hold values from -6 to 6
- out_weight: bfloat16 [128, 8, 1024], P(None, 'head'), may hold values from -0.1875 to 0.1875
- log_decay: float32 [2, 8, 8192], P('dp', 'head', 'ctx'), may hold values from -1 to 0, as said below
- level_gates: float32 [2, 8, 8, 8192], P('dp', 'head', None, 'ctx'), may hold values from 0.25 to 2
Outputs:
- query_grad: bfloat16 [2, 8192, 1024], P('dp', 'ctx', 'head')
- key_grad: bfloat16 [2, 8192, 1024], P('dp', 'ctx', 'head')
- value_grad: bfloat16 [2, 8192, 1024], P('dp', 'ctx', 'head')
- decay_grad: float32 [2, 8, 8192], P('dp', 'head', 'ctx')
- gate_grad: float32 [2, 8, 8, 8192], P('dp', 'head', None, 'ctx')
- weight_grad: float32 [128, 8, 1024], P(('dp', 'ctx'), 'head')
The draws below stay inside these ranges and needn't reach their ends.
Inputs may be any that keep to these rules, and one draw needn't show every extreme that they name: `log_decay`: log-decays of every position and head are nonpositive.
All inputs are finite; a program needn't handle non-finite values.
Results may differ from the reference program's by a relative error of at most 0.012.
The reference program's roundings to bfloat16 on the way count: a program that leaves them out, or rounds other values in their place, can miss the bound.
Values sent between devices are 32-bit elements; how exact they have to be, the bound alone decides.
A program may use at most 64 MiB of HBM per device.

```python
import math
import jax
import jax.numpy as jnp
from jax import lax

D = 1024
HEAD_TOTAL = 8
DH = 128
TOK_DEV = 256
SEQUENCE_COUNT = 2
SEQUENCE_LENGTH = 8192
LOCAL_BITS = 2
CTX_BITS = 5
LEVELS = 8
N_CTX = 32


def draw_log_decay(key, part):
    every_key = jax.random.split(key, 7)
    full_shape = (SEQUENCE_COUNT, HEAD_TOTAL, SEQUENCE_LENGTH)
    pick_draw = jax.random.uniform(every_key[0], (SEQUENCE_COUNT, HEAD_TOTAL, 1))
    fast_rate = jax.random.uniform(every_key[1], (SEQUENCE_COUNT, HEAD_TOTAL, 1), minval=0.02, maxval=0.0333)
    slow_rate = jax.random.uniform(every_key[2], (SEQUENCE_COUNT, HEAD_TOTAL, 1), minval=0.05, maxval=0.3) * (2.3 / SEQUENCE_LENGTH)
    fast_share = 0.5
    small_noise = jax.random.uniform(every_key[3], full_shape, minval=0.5, maxval=1.5)
    per_head_rate = jnp.where(pick_draw < fast_share, fast_rate, slow_rate)
    spread = jnp.exp(jax.random.uniform(every_key[4], (SEQUENCE_COUNT, HEAD_TOTAL, SEQUENCE_LENGTH // TOK_DEV, 1), minval=-0.7, maxval=0.7))
    small_noise = (small_noise.reshape(SEQUENCE_COUNT, HEAD_TOTAL, SEQUENCE_LENGTH // TOK_DEV, TOK_DEV) * spread).reshape(full_shape)
    spike_positions = jax.random.randint(every_key[5], (SEQUENCE_COUNT, HEAD_TOTAL, 2, 1), 0, SEQUENCE_LENGTH)
    spike_depth = jnp.log(jax.random.uniform(every_key[6], (SEQUENCE_COUNT, HEAD_TOTAL, 2, 1), minval=0.5, maxval=0.8))
    spike_mask = jnp.arange(SEQUENCE_LENGTH, dtype=jnp.int32)[None, None, None, :] == spike_positions
    spike_log_value = jnp.sum(jnp.where(spike_mask, spike_depth, 0.0), axis=2)
    return (-per_head_rate * small_noise + spike_log_value).astype(jnp.float32)


def level_of(rng, shape, cuts, low, largest):
    gain = 1.0
    for position, parts in cuts:
        steps = jax.random.uniform(jax.random.fold_in(jax.random.fold_in(rng, 6), position), (parts,), jnp.float32, low / len(cuts), largest / len(cuts))
        gain = gain * jnp.repeat(jnp.exp(steps), shape[position] // parts).reshape((-1,) + (1,) * (len(shape) - 1 - position))
    return gain


def gaussian(key, shape, scale, limit, cuts=(), kind=jnp.bfloat16):
    values = jax.random.normal(key, shape, jnp.float32) * scale
    if len(cuts) > 0:
        values = level_of(key, shape, cuts, -0.22, 0.18) * values
    return jnp.clip(values, min=-limit, max=limit).astype(kind)


def setup_inputs(seed: int = 0) -> dict:
    arg_keys = jax.random.split(jax.random.key(seed), 8)
    queries = gaussian(arg_keys[0], (SEQUENCE_COUNT, SEQUENCE_LENGTH, HEAD_TOTAL * DH), 0.0884, 0.59765625, ((0, 2), (1, 32), (2, 4)))
    key_vectors = gaussian(arg_keys[1], (SEQUENCE_COUNT, SEQUENCE_LENGTH, HEAD_TOTAL * DH), 0.0884, 0.59765625, ((0, 2), (1, 32), (2, 4)))
    value_vectors = gaussian(arg_keys[2], (SEQUENCE_COUNT, SEQUENCE_LENGTH, HEAD_TOTAL * DH), 0.0884, 0.59765625, ((0, 2), (1, 32), (2, 4)))
    out_cotangent = gaussian(arg_keys[3], (SEQUENCE_COUNT, SEQUENCE_LENGTH, D), 1.0, 6.0, ((0, 2), (1, 32)))
    out_weight = gaussian(arg_keys[4], (DH, HEAD_TOTAL, D), (HEAD_TOTAL * DH) ** -0.5, 0.1875, ((1, 4),))
    log_decay = draw_log_decay(jax.random.fold_in(arg_keys[7], 71), 0)
    level_gates = jnp.clip(jnp.exp(math.log(2.0) - 2.0794415 * jax.random.uniform(arg_keys[6], (SEQUENCE_COUNT, HEAD_TOTAL, LEVELS, SEQUENCE_LENGTH), jnp.float32) ** level_of(arg_keys[6], (SEQUENCE_COUNT, HEAD_TOTAL, LEVELS, SEQUENCE_LENGTH), ((0, 2), (1, 4), (3, 32)), -0.2, 0.2)), 0.25, 2.0)
    return dict(queries=queries, key_vectors=key_vectors, value_vectors=value_vectors, out_cotangent=out_cotangent, out_weight=out_weight, log_decay=log_decay, level_gates=level_gates)


def bit_count(values, shifts):
    running = jnp.zeros_like(values)
    for shift_by in range(shifts):
        running = running + (jnp.right_shift(values, shift_by) > 0).astype(jnp.int32)
    return running


def level_table(row_count, local_bits):
    span_len = row_count // (2 ** local_bits)
    span_ids = jnp.arange(row_count, dtype=jnp.int32) // span_len
    return bit_count(jnp.bitwise_xor(span_ids[:, None], span_ids[None, :]), local_bits)


def phase_a(key_rows, value_rows, decay_rows):
    cumulative = jnp.cumsum(decay_rows)
    to_end = jnp.exp(cumulative[-1] - cumulative)
    scaled = (to_end[:, None] * value_rows.astype(jnp.float32)).astype(jnp.bfloat16)
    state_rows = jnp.dot(key_rows.T, scaled, preferred_element_type=jnp.float32)
    return state_rows, cumulative[-1]


def phase_b(query_rows, key_rows, value_rows, grad_rows, decay_rows, gate_rows, arriving, local_bits):
    row_count = query_rows.shape[0]
    cumulative = jnp.cumsum(decay_rows)
    levels = level_table(row_count, local_bits)
    positions = jnp.arange(row_count, dtype=jnp.int32)
    causal = positions[:, None] >= positions[None, :]
    log_gap = cumulative[:, None] - cumulative[None, :]
    decay_mat = jnp.where(causal, jnp.exp(jnp.where(causal, log_gap, 0.0)), 0.0)
    picked = jnp.zeros((row_count, row_count), jnp.float32)
    for level_id in range(local_bits + 1):
        picked = picked + jnp.where(levels == level_id, gate_rows[level_id][:, None], 0.0)
    mixing = picked * decay_mat
    scores = jnp.dot(query_rows, key_rows.T, preferred_element_type=jnp.float32)
    weights = mixing * scores
    weights_low = weights.astype(jnp.bfloat16)
    state_low = arriving.astype(jnp.bfloat16)
    grad_float = grad_rows.astype(jnp.float32)
    projected = jnp.einsum("tc,mce->mte", query_rows.astype(jnp.float32), state_low.astype(jnp.float32))
    lift_coef = gate_rows[local_bits + 1:] * jnp.exp(cumulative)[None, :]
    attended = jnp.dot(weights_low, value_rows, preferred_element_type=jnp.float32)
    attended = attended + jnp.sum(lift_coef[:, :, None] * projected, 0)
    attended_low = attended.astype(jnp.bfloat16)
    grad_weights = jnp.dot(grad_rows, value_rows.T, preferred_element_type=jnp.float32)
    value_local = jnp.dot(weights_low.T, grad_rows, preferred_element_type=jnp.float32)
    score_grad = (grad_weights * mixing).astype(jnp.bfloat16)
    query_grad = jnp.dot(score_grad, key_rows, preferred_element_type=jnp.float32)
    key_local = jnp.dot(score_grad.T, query_rows, preferred_element_type=jnp.float32)
    plain_terms = grad_weights * scores * decay_mat
    pair_terms = plain_terms * picked
    gate_local = jnp.stack([jnp.sum(jnp.where(levels == level_id, plain_terms, 0.0), 1) for level_id in range(local_bits + 1)])
    row_terms = jnp.sum(pair_terms, 1)
    col_terms = jnp.sum(pair_terms, 0)
    inner_prod = jnp.sum(projected * grad_float[None], 2)
    gate_far = jnp.exp(cumulative)[None, :] * inner_prod
    row_terms = row_terms + jnp.sum(lift_coef * inner_prod, 0)
    back_rows = jnp.einsum("te,mce->mtc", grad_float, state_low.astype(jnp.float32))
    query_grad = query_grad + jnp.sum(lift_coef[:, :, None] * back_rows, 0)
    lifted = (lift_coef[:, :, None] * grad_float[None]).astype(jnp.bfloat16)
    query_states = jnp.einsum("tc,mte->mce", query_rows.astype(jnp.float32), lifted.astype(jnp.float32))
    gate_grad = jnp.concatenate([gate_local, gate_far], 0)
    return attended_low, query_grad, key_local, value_local, gate_grad, row_terms, col_terms, query_states


def phase_c(key_rows, value_rows, decay_rows, returned, key_local, value_local, row_terms, col_terms):
    cumulative = jnp.cumsum(decay_rows)
    to_end = jnp.exp(cumulative[-1] - cumulative)
    state_low = returned.astype(jnp.bfloat16)
    key_far = to_end[:, None] * jnp.dot(value_rows, state_low.T, preferred_element_type=jnp.float32)
    value_far = to_end[:, None] * jnp.dot(key_rows, state_low, preferred_element_type=jnp.float32)
    col_total = col_terms + jnp.sum(key_rows.astype(jnp.float32) * key_far, 1)
    return key_local + key_far, value_local + value_far, row_terms - col_total


def link_weights(totals, ctx_bits):
    block_count = totals.shape[0]
    before = jnp.cumsum(totals, 0) - totals
    block_ids = jnp.arange(block_count, dtype=jnp.int32)
    relation = bit_count(jnp.bitwise_xor(block_ids[:, None], block_ids[None, :]), ctx_bits)
    is_lower = block_ids[None, :] < block_ids[:, None]
    log_gap = before[:, None, :] - before[None, :, :] - totals[None, :, :]
    scaling = jnp.where(is_lower[:, :, None], jnp.exp(jnp.where(is_lower[:, :, None], log_gap, 0.0)), 0.0)
    level_ids = jnp.arange(1, ctx_bits + 1, dtype=jnp.int32)
    chosen = ((relation[:, :, None] == level_ids[None, None, :]) & is_lower[:, :, None]).astype(jnp.float32)
    return chosen[:, :, :, None] * scaling[:, :, None, :]


def reference(queries, key_vectors, value_vectors, out_cotangent, out_weight, log_decay, level_gates):
    local_bits = LOCAL_BITS
    ctx_bits = CTX_BITS
    block_count = N_CTX
    row_count = TOK_DEV
    flat = HEAD_TOTAL * block_count
    weight_total = jnp.zeros((DH, HEAD_TOTAL, D), jnp.float32)
    query_out, key_out, value_out, decay_out, gate_out = [], [], [], [], []
    for seq_index in range(SEQUENCE_COUNT):
        def heads_major(array):
            return array[seq_index].reshape(block_count, row_count, HEAD_TOTAL, DH).transpose(2, 0, 1, 3).reshape(flat, row_count, DH)

        query_rows = heads_major(queries)
        key_rows = heads_major(key_vectors)
        value_rows = heads_major(value_vectors)
        grad_full = jnp.einsum("td,chd->htc", out_cotangent[seq_index].astype(jnp.float32), out_weight.astype(jnp.float32)).astype(jnp.bfloat16)
        grad_rows = grad_full.reshape(flat, row_count, DH)
        decay_rows = log_decay[seq_index].reshape(flat, row_count)
        gate_rows = level_gates[seq_index].reshape(HEAD_TOTAL, LEVELS, block_count, row_count).transpose(0, 2, 1, 3).reshape(flat, LEVELS, row_count)
        states, totals = lax.map(lambda packed: phase_a(*packed), (key_rows, value_rows, decay_rows))
        weights = link_weights(totals.reshape(HEAD_TOTAL, block_count).T, ctx_bits)
        arriving = jnp.einsum("rqmh,hqab->hrmab", weights, states.reshape(HEAD_TOTAL, block_count, DH, DH), precision=lax.Precision.HIGHEST)
        arriving = arriving.reshape(flat, ctx_bits, DH, DH)
        results = lax.map(lambda packed: phase_b(*packed, local_bits), (query_rows, key_rows, value_rows, grad_rows, decay_rows, gate_rows, arriving))
        attended, query_grad, key_local, value_local, gate_grad, row_terms, col_terms, query_states = results
        returned = jnp.einsum("rqmh,hrmab->hqab", weights, query_states.reshape(HEAD_TOTAL, block_count, ctx_bits, DH, DH), precision=lax.Precision.HIGHEST)
        returned = returned.reshape(flat, DH, DH)
        key_grad, value_grad, flow = lax.map(lambda packed: phase_c(*packed), (key_rows, value_rows, decay_rows, returned, key_local, value_local, row_terms, col_terms))
        flow = flow.reshape(HEAD_TOTAL, block_count * row_count)
        decay_out.append(jnp.flip(jnp.cumsum(jnp.flip(flow, 1), 1), 1))
        attended_full = attended.reshape(HEAD_TOTAL, block_count * row_count, DH)
        weight_total = weight_total + jnp.einsum("htc,td->chd", attended_full.astype(jnp.float32), out_cotangent[seq_index].astype(jnp.float32))

        def token_major(array):
            return array.reshape(HEAD_TOTAL, block_count * row_count, DH).transpose(1, 0, 2).reshape(block_count * row_count, HEAD_TOTAL * DH).astype(jnp.bfloat16)

        query_out.append(token_major(query_grad))
        key_out.append(token_major(key_grad))
        value_out.append(token_major(value_grad))
        gate_out.append(gate_grad.reshape(HEAD_TOTAL, block_count, LEVELS, row_count).transpose(0, 2, 1, 3).reshape(HEAD_TOTAL, LEVELS, block_count * row_count))
    return (jnp.stack(query_out), jnp.stack(key_out), jnp.stack(value_out), jnp.stack(decay_out), jnp.stack(gate_out), weight_total)
```

```python
import jax
import jax.numpy as jnp
from jax import lax
from jax.experimental import pallas as pl
from jax.experimental.pallas import tpu as pltpu
from jax.sharding import PartitionSpec as P

F32 = jnp.float32
BF16 = jnp.bfloat16
MESH = pl.DeviceIdType.MESH
NZ = 8
NY = 4
ROWS = 256
DH = 128
SPAN = 64
FAR = 5

NN = (((1,), (0,)), ((), ()))
NT = (((1,), (1,)), ((), ()))
TN = (((0,), (0,)), ((), ()))


def dot(a, b, dims):
    return lax.dot_general(a, b, dims, preferred_element_type=F32)


def iota(shape, dim):
    return lax.broadcasted_iota(jnp.int32, shape, dim)


def exact_dot(x, ones):
    hi = x.astype(BF16)
    rest = x - hi.astype(F32)
    mid = rest.astype(BF16)
    low = (rest - mid.astype(F32)).astype(BF16)
    return dot(hi, ones, NN) + dot(mid, ones, NN) + dot(low, ones, NN)


D_ROW = 0
D_COL = D_ROW + 8
F_ROW = D_COL + 4
F_COL = F_ROW + 8
S_UP = F_COL + 4
S_DOWN = S_UP + 8
T_UP = S_DOWN + 8
T_DOWN = T_UP + 4
Q_STEP = T_DOWN + 4
R_UP = Q_STEP + 10
R_DOWN = R_UP + 8
W_DP = R_DOWN + 8
W_Y = W_DP + 1
W_Z = W_Y + 6
COPIES = W_Z + 8


def kernel(
    q_ref, k_ref, v_ref, cot_ref, ow_ref, decay_ref, gates_ref,
    qg_ref, kg_ref, vg_ref, dg_ref, gg_ref, wg_ref,
    x_ref, xt_ref, zc_ref, zt_ref, flow_ref,
    dbuf, dcol, fbuf, fcol, etab, ctab,
    sbuf, tbuf, qs_ref, qa, qb, qc, qb2, qc2, pbuf, rsend, rrecv,
    g_ref, lifted_ref, lev_ref, attl_ref, qloc, kloc, vloc, att_ref,
    wbuf, wdp, usum, wa1, wb1, wa2, wb2, sa2, sb2, zsum, wz,
    ssem, rsem,
):
    ctx = lax.axis_index("ctx")
    dp = lax.axis_index("dp")
    y = lax.div(ctx, NZ)
    z = lax.rem(ctx, NZ)

    def zz(j):
        return lax.rem(z + j + NZ, NZ)

    def yy(j):
        return lax.rem(y + j + NY, NY)

    def at_z(j):
        return {"ctx": y * NZ + zz(j)}

    def at_y(j):
        return {"ctx": yy(j) * NZ + z}

    other = {"dp": 1 - dp}
    sent = []

    def copy(src, dst, n, where):
        return pltpu.make_async_remote_copy(
            src_ref=src, dst_ref=dst, send_sem=ssem.at[n], recv_sem=rsem.at[n],
            device_id=where, device_id_type=MESH,
        )

    def send(src, dst, n, where):
        c = copy(src, dst, n, where)
        c.start()
        sent.append(c)

    def arrived(dst, n, where):
        copy(dst, dst, n, where).wait_recv()

    barrier = pltpu.get_barrier_semaphore()
    for j in range(1, NZ):
        pl.semaphore_signal(barrier, inc=1, device_id=at_z(j), device_id_type=MESH)
    for j in range(1, NY):
        pl.semaphore_signal(barrier, inc=1, device_id=at_y(j), device_id_type=MESH)
    pl.semaphore_signal(barrier, inc=1, device_id=other, device_id_type=MESH)

    x_ref[...] = jnp.zeros_like(x_ref)
    x_ref[0:16, :] = gates_ref[...]
    x_ref[16:18, :] = decay_ref[...]
    upto = (iota((ROWS, ROWS), 0) <= iota((ROWS, ROWS), 1)).astype(BF16)
    cum = exact_dot(x_ref[16:24, :], upto)
    x_ref[24:32, :] = cum
    xt_ref[...] = jnp.transpose(x_ref[...])
    total = jnp.broadcast_to(cum[:, ROWS - 1 : ROWS], (8, 128))
    dbuf[pl.ds(z, 1)] = total[None]

    def cols(h):
        return slice(h * DH, (h + 1) * DH)

    def cum_col(h):
        return xt_ref[:, 24 + h : 25 + h]

    def to_end(h):
        return jnp.exp(x_ref[24 + h : 25 + h, ROWS - 1 : ROWS] - cum_col(h))

    def lift(h, m):
        return xt_ref[:, h * 8 + 3 + m : h * 8 + 4 + m] * jnp.exp(cum_col(h))

    for h in range(2):
        scaled = (to_end(h) * v_ref[:, cols(h)].astype(F32)).astype(BF16)
        sbuf[pl.ds(z, 1), h] = dot(k_ref[:, cols(h)], scaled, TN)[None]

    pl.semaphore_wait(barrier, NZ - 1 + NY - 1 + 1)

    for j in range(1, NZ):
        send(dbuf.at[z], dbuf.at[z], D_ROW + j, at_z(j))
    for h in range(2):
        send(sbuf.at[z, h], sbuf.at[z, h], S_UP + h, at_z(1))
        send(sbuf.at[z, h], sbuf.at[z, h], S_DOWN + h, at_z(-1))

    mixed = dot(cot_ref[...], ow_ref[...], NT).astype(BF16)
    ri, ci = iota((ROWS, ROWS), 0), iota((ROWS, ROWS), 1)
    perm = (ri == 2 * (ci & (DH - 1)) + jnp.right_shift(ci, 7)).astype(BF16)
    g_ref[...] = dot(mixed, perm, NN).astype(BF16)

    def make_qs(h):
        g = g_ref[:, cols(h)].astype(F32)
        for m in range(FAR):
            lifted_ref[h, :, m * DH : (m + 1) * DH] = (lift(h, m) * g).astype(BF16)
        allq = dot(q_ref[:, cols(h)], lifted_ref[h], TN)
        for m in range(FAR):
            qs_ref[h, m] = allq[:, m * DH : (m + 1) * DH]

    for h in range(2):
        make_qs(h)
        send(qs_ref.at[h, 4], qc.at[h], Q_STEP + h, at_y(-1))
        send(qs_ref.at[h, 4], qb.at[h], Q_STEP + 2 + h, at_y(1))
        send(qs_ref.at[h, 3], qa.at[h], Q_STEP + 4 + h, at_y(-1))

    for j in range(1, NZ):
        arrived(dbuf.at[zz(-j)], D_ROW + j, at_z(j))
    zero = jnp.zeros((8, 128), F32)
    running = zero
    before = []
    mine = zero
    for i in range(NZ):
        before.append(running)
        d = dbuf[i]
        mine = mine + jnp.where(i < z, d, zero)
        running = running + d
    row_total = running
    for i in range(NZ):
        after = before[i] + dbuf[i]
        etab[i] = jnp.exp(row_total - after)
        low = i < z
        ctab[i] = jnp.where(low, jnp.exp(jnp.where(low, mine - after, zero)), zero)
    dcol[pl.ds(y, 1), 0:8, :] = row_total[None]
    dcol[pl.ds(y, 1), 8:16, :] = mine[None]
    for j in range(1, NY):
        send(dcol.at[y], dcol.at[y], D_COL + j, at_y(j))

    def gather_step(k):
        for h in range(2):
            if k < 3 or h == 0:
                arrived(sbuf.at[zz(-k), h], S_UP + 2 * (k - 1) + h, at_z(1))
                send(sbuf.at[zz(-k), h], sbuf.at[zz(-k), h], S_UP + 2 * k + h, at_z(1))
            if k < 3 or h == 1:
                arrived(sbuf.at[zz(k), h], S_DOWN + 2 * (k - 1) + h, at_z(-1))
                send(sbuf.at[zz(k), h], sbuf.at[zz(k), h], S_DOWN + 2 * k + h, at_z(-1))

    def attend(h):
        q, k, v, g = q_ref[:, cols(h)], k_ref[:, cols(h)], v_ref[:, cols(h)], g_ref[:, cols(h)]
        rows, columns = iota((ROWS, ROWS), 0), iota((ROWS, ROWS), 1)
        causal = rows >= columns
        split = jnp.bitwise_xor(jnp.right_shift(rows, 6), jnp.right_shift(columns, 6))
        gap = cum_col(h) - x_ref[24 + h : 25 + h, :]
        decay = jnp.where(causal, jnp.exp(jnp.where(causal, gap, 0.0)), 0.0)
        gate = [xt_ref[:, h * 8 + l : h * 8 + l + 1] for l in range(3)]
        picked = jnp.where(split == 0, gate[0], jnp.where(split == 1, gate[1], gate[2]))
        mixing = picked * decay
        scores = dot(q, k, NT)
        gw = dot(g, v, NT)
        weights = (mixing * scores).astype(BF16)
        sg = gw * mixing
        sg_low = sg.astype(BF16)
        attl_ref[h] = dot(weights, v, NN)
        vloc[h] = dot(weights, g, TN)
        qloc[h] = dot(sg_low, k, NN)
        kloc[h] = dot(sg_low, q, TN)
        flow_ref[h : h + 1, :] = jnp.sum(sg * scores, 0, keepdims=True)
        plain = gw * scores * decay
        near = jnp.zeros((ROWS, 1), F32)
        for l in range(3):
            hit = (split == l) if l < 2 else (split >= 2)
            part = jnp.sum(jnp.where(hit, plain, 0.0), 1, keepdims=True)
            zc_ref[:, h * 8 + l : h * 8 + l + 1] = part
            near = near + gate[l] * part
        zc_ref[:, 16 + h : 17 + h] = near

    zc_ref[...] = jnp.zeros_like(zc_ref)
    flow_ref[...] = jnp.zeros_like(flow_ref)
    gather_step(1)
    attend(0)
    gather_step(2)
    for h in range(2):
        arrived(qc.at[h], Q_STEP + h, at_y(-1))
        send(qc.at[h], qc2.at[h], Q_STEP + 6 + h, at_y(-1))
        arrived(qb.at[h], Q_STEP + 2 + h, at_y(1))
        send(qb.at[h], qb2.at[h], Q_STEP + 8 + h, at_y(1))
    attend(1)
    gather_step(3)

    for j in range(1, NY):
        arrived(dcol.at[yy(-j)], D_COL + j, at_y(j))
    row1, row2 = dcol[1, 0:8, :], dcol[2, 0:8, :]
    w2, w3 = jnp.exp(dcol[2, 8:16, :]), jnp.exp(dcol[3, 8:16, :])
    wnext = jnp.exp(dcol[yy(1), 8:16, :])
    ca = jnp.where(lax.rem(y, 2) == 0, wnext, zero)
    cb = jnp.where(y == 0, w3 * jnp.exp(row1 + row2), zero)
    cb2 = jnp.where(y == 1, w3 * jnp.exp(row2), zero)
    cc = jnp.where(y == 1, w2, zero)
    cc2 = jnp.where(y == 0, w2 * jnp.exp(row1), zero)
    for h in range(2):
        arrived(qa.at[h], Q_STEP + 4 + h, at_y(-1))
        arrived(qc2.at[h], Q_STEP + 6 + h, at_y(-1))
        arrived(qb2.at[h], Q_STEP + 8 + h, at_y(1))
        s = slice(h, h + 1)
        pbuf[h] = (
            ca[s] * qa[h] + cb[s] * qb[h] + cb2[s] * qb2[h] + cc[s] * qc[h] + cc2[s] * qc2[h]
        )

    def contribution(h, target):
        e = etab[target, h : h + 1, :]
        c = ctab[target, h : h + 1, :]
        none = jnp.zeros_like(c)
        far = lax.div(target, 4) != lax.div(z, 4)
        same = lax.div(target, 2) == lax.div(z, 2)
        c3 = jnp.where(far, c, none)
        c1 = jnp.where(same, c, none)
        c2 = c - c3 - c1
        return e * pbuf[h] + c1 * qs_ref[h, 0] + c2 * qs_ref[h, 1] + c3 * qs_ref[h, 2]

    def reduce_step(k):
        for h in range(2):
            for up in (0, 1):
                first = 0 if h == 1 - up else 1
                if k < first:
                    continue
                sign = 1 if up else -1
                base = R_UP if up else R_DOWN
                mine_part = contribution(h, zz(sign * (4 - k)))
                if k > first:
                    arrived(rrecv.at[up, h, k - 1], base + 2 * (k - 1) + h, at_z(sign))
                    mine_part = mine_part + rrecv[up, h, k - 1]
                rsend[up, h, k] = mine_part
                send(rsend.at[up, h, k], rrecv.at[up, h, k], base + 2 * k + h, at_z(sign))

    reduce_step(0)

    for h in range(2):
        for k in range(1, 5):
            if k == 4:
                if h == 0:
                    arrived(sbuf.at[zz(-4), h], S_UP + 6 + h, at_z(1))
                else:
                    arrived(sbuf.at[zz(4), h], S_DOWN + 6 + h, at_z(-1))
                continue
            if k == 3:
                if h == 1:
                    arrived(sbuf.at[zz(-3), h], S_UP + 4 + h, at_z(1))
                else:
                    arrived(sbuf.at[zz(3), h], S_DOWN + 4 + h, at_z(-1))
        lev = [jnp.zeros((DH, DH), F32) for _ in range(3)]
        whole = jnp.zeros((DH, DH), F32)
        for i in range(NZ):
            s = sbuf[i, h]
            c = ctab[i, h : h + 1, :]
            none = jnp.zeros_like(c)
            far = lax.div(z, 4) != i // 4
            same = lax.div(z, 2) == i // 2
            c3 = jnp.where(far, c, none)
            c1 = jnp.where(same, c, none)
            c2 = c - c3 - c1
            lev[0] = lev[0] + c1 * s
            lev[1] = lev[1] + c2 * s
            lev[2] = lev[2] + c3 * s
            whole = whole + etab[i, h : h + 1, :] * s
        for m in range(3):
            lev_ref[h, :, m * DH : (m + 1) * DH] = lev[m].astype(BF16)
        tbuf[pl.ds(y, 1), h] = whole[None]
        send(tbuf.at[y, h], tbuf.at[y, h], T_UP + h, at_y(1))
        send(tbuf.at[y, h], tbuf.at[y, h], T_DOWN + h, at_y(-1))

    reduce_step(1)
    arrived(tbuf.at[yy(-1), 0], T_UP + 0, at_y(1))
    send(tbuf.at[yy(-1), 0], tbuf.at[yy(-1), 0], T_UP + 2, at_y(1))
    arrived(tbuf.at[yy(1), 1], T_DOWN + 1, at_y(-1))
    send(tbuf.at[yy(1), 1], tbuf.at[yy(1), 1], T_DOWN + 2, at_y(-1))
    arrived(tbuf.at[yy(-1), 1], T_UP + 1, at_y(1))
    arrived(tbuf.at[yy(1), 0], T_DOWN + 0, at_y(-1))
    reduce_step(2)
    arrived(tbuf.at[yy(-2), 0], T_UP + 2, at_y(1))
    arrived(tbuf.at[yy(2), 1], T_DOWN + 2, at_y(-1))

    f4 = jnp.where(lax.rem(y, 2) == 1, jnp.exp(mine), zero)
    f5 = jnp.where(y >= 2, jnp.exp(mine + jnp.where(y == 3, row2, zero)), zero)
    f5low = f5 * jnp.exp(row1)

    def far_rows(h):
        s = slice(h, h + 1)
        lev_ref[h, :, 3 * DH : 4 * DH] = (f4[s] * tbuf[yy(-1), h]).astype(BF16)
        lev_ref[h, :, 4 * DH : 5 * DH] = (f5[s] * tbuf[1, h] + f5low[s] * tbuf[0, h]).astype(BF16)
        projected = dot(q_ref[:, cols(h)], lev_ref[h], NN)
        g = g_ref[:, cols(h)].astype(F32)
        attended = attl_ref[h]
        extra = zc_ref[:, 16 + h : 17 + h]
        ecum = jnp.exp(cum_col(h))
        for m in range(FAR):
            part = projected[:, m * DH : (m + 1) * DH]
            coef = lift(h, m)
            attended = attended + coef * part
            inner = jnp.sum(part * g, 1, keepdims=True)
            zc_ref[:, h * 8 + 3 + m : h * 8 + 4 + m] = ecum * inner
            extra = extra + coef * inner
        zc_ref[:, 16 + h : 17 + h] = extra
        att_ref[:, cols(h)] = attended.astype(BF16)

    for h in range(2):
        far_rows(h)

    r, j = iota((512, ROWS), 0), iota((512, ROWS), 1)
    wanted = (r & 1) * DH + jnp.right_shift(r, 3) * 2 + (jnp.right_shift(r, 1) & 1)
    half = jnp.right_shift(r, 2) & 1
    match = wanted == j
    first_half = jnp.where(match & (half == 0), 1.0, 0.0).astype(BF16)
    second_half = jnp.where(match & (half == 1), 1.0, 0.0).astype(BF16)
    att = att_ref[...]
    lhs0 = dot(first_half, att, NT).astype(BF16)
    lhs1 = dot(second_half, att, NT).astype(BF16)
    wbuf[...] = dot(lhs0, cot_ref[:, 0:512], NN) + dot(lhs1, cot_ref[:, 512:1024], NN)
    theirs = pl.multiple_of((1 - dp) * 256, 256)
    ours = pl.multiple_of(dp * 256, 256)
    send(wbuf.at[pl.ds(theirs, 256)], wdp, W_DP, other)

    reduce_step(3)
    for h in range(2):
        qfar = dot(lifted_ref[h], lev_ref[h], NT)
        qg_ref[:, cols(h)] = (qloc[h] + qfar).astype(BF16)

    arrived(wdp, W_DP, other)
    usum[...] = wbuf[pl.ds(ours, 256), :] + wdp[...]

    def chunk(jy, start):
        return pl.ds(pl.multiple_of(yy(jy) * 64 + start, 32), 32)

    send(usum.at[chunk(2, 0)], wa1, W_Y + 0, at_y(1))
    send(usum.at[chunk(-2, 32)], wb1, W_Y + 1, at_y(-1))
    send(usum.at[chunk(1, 32)], wa2.at[pl.ds(32, 32)], W_Y + 2, at_y(1))
    send(usum.at[chunk(-1, 0)], wb2.at[pl.ds(0, 32)], W_Y + 3, at_y(-1))

    zt_ref[...] = jnp.transpose(zc_ref[...])
    gg_ref[...] = zt_ref[0:16, :]
    for h in range(2):
        arrived(rrecv.at[1, h, 3], R_UP + 6 + h, at_z(1))
        arrived(rrecv.at[0, h, 3], R_DOWN + 6 + h, at_z(-1))
        e = etab[z, h : h + 1, :]
        returned = (e * pbuf[h] + rrecv[1, h, 3] + rrecv[0, h, 3]).astype(BF16)
        k, v = k_ref[:, cols(h)], v_ref[:, cols(h)]
        w = to_end(h)
        kfar = w * dot(v, returned, NT)
        vfar = w * dot(k, returned, NN)
        kg_ref[:, cols(h)] = (kloc[h] + kfar).astype(BF16)
        vg_ref[:, cols(h)] = (vloc[h] + vfar).astype(BF16)
        zc_ref[:, 24 + h : 25 + h] = jnp.sum(k.astype(F32) * kfar, 1, keepdims=True)

    arrived(wa1, W_Y + 0, at_y(1))
    sa2[...] = usum[chunk(1, 0), :] + wa1[...]
    send(sa2, wa2.at[pl.ds(0, 32)], W_Y + 4, at_y(1))
    arrived(wb1, W_Y + 1, at_y(-1))
    sb2[...] = usum[chunk(-1, 32), :] + wb1[...]
    send(sb2, wb2.at[pl.ds(32, 32)], W_Y + 5, at_y(-1))

    back = jnp.transpose(zc_ref[...])
    flow = zt_ref[16:24, :] - flow_ref[...] - back[24:32, :]
    block_flow = jnp.broadcast_to(jnp.sum(flow, 1, keepdims=True), (8, 128))
    fbuf[pl.ds(z, 1)] = block_flow[None]
    for jz in range(1, NZ):
        send(fbuf.at[z], fbuf.at[z], F_ROW + jz, at_z(jz))
    onward = (iota((ROWS, ROWS), 0) >= iota((ROWS, ROWS), 1)).astype(BF16)
    within = exact_dot(flow, onward)

    arrived(wa2.at[pl.ds(32, 32)], W_Y + 2, at_y(1))
    arrived(wb2.at[pl.ds(0, 32)], W_Y + 3, at_y(-1))
    arrived(wa2.at[pl.ds(0, 32)], W_Y + 4, at_y(1))
    arrived(wb2.at[pl.ds(32, 32)], W_Y + 5, at_y(-1))
    own = pl.ds(pl.multiple_of(y * 64, 64), 64)
    zsum[...] = usum[own, :] + wa2[...] + wb2[...]

    def part_of(jz):
        return pl.ds(pl.multiple_of(zz(jz) * 8, 8), 8)

    for jz in range(1, NZ):
        send(zsum.at[part_of(jz)], wz.at[jz], W_Z + jz, at_z(jz))

    tail = zero
    row_flow = zero
    for jz in range(1, NZ):
        arrived(fbuf.at[zz(-jz)], F_ROW + jz, at_z(jz))
    for i in range(NZ):
        f = fbuf[i]
        row_flow = row_flow + f
        tail = tail + jnp.where(i > z, f, zero)
    fcol[pl.ds(y, 1)] = row_flow[None]
    for jy in range(1, NY):
        send(fcol.at[y], fcol.at[y], F_COL + jy, at_y(jy))

    result = zsum[part_of(0), :]
    for jz in range(1, NZ):
        arrived(wz.at[jz], W_Z + jz, at_z(jz))
        result = result + wz[jz]
    wg_ref[:, 0:512] = result[0:4, :]
    wg_ref[:, 512:1024] = result[4:8, :]

    for jy in range(1, NY):
        arrived(fcol.at[yy(-jy)], F_COL + jy, at_y(jy))
    for i in range(NY):
        tail = tail + jnp.where(i > y, fcol[i], zero)
    dg_ref[...] = (within + tail[:, 0:1])[0:2, :]

    for c in sent:
        c.wait_send()


def local(queries, key_vectors, value_vectors, out_cotangent, out_weight, log_decay, level_gates):
    v32 = lambda *s: pltpu.VMEM(s, F32)
    v16 = lambda *s: pltpu.VMEM(s, BF16)
    vmem = pl.BlockSpec(memory_space=pltpu.VMEM)
    scratch = [
        v32(128, ROWS), v32(ROWS, 128), v32(ROWS, 128), v32(128, ROWS), v32(8, ROWS),
        v32(NZ, 8, 128), v32(NY, 16, 128), v32(NZ, 8, 128), v32(NY, 8, 128),
        v32(NZ, 8, 128), v32(NZ, 8, 128),
        v32(NZ, 2, DH, DH), v32(NY, 2, DH, DH), v32(2, FAR, DH, DH),
        v32(2, DH, DH), v32(2, DH, DH), v32(2, DH, DH), v32(2, DH, DH), v32(2, DH, DH),
        v32(2, DH, DH), v32(2, 2, 4, DH, DH), v32(2, 2, 4, DH, DH),
        v16(ROWS, 256), v16(2, ROWS, FAR * DH), v16(2, DH, FAR * DH), v32(2, ROWS, DH),
        v32(2, ROWS, DH), v32(2, ROWS, DH), v32(2, ROWS, DH), v16(ROWS, 256),
        v32(512, 512), v32(256, 512), v32(256, 512), v32(32, 512), v32(32, 512),
        v32(64, 512), v32(64, 512), v32(32, 512), v32(32, 512), v32(64, 512), v32(NZ, 8, 512),
        pltpu.SemaphoreType.DMA((COPIES,)), pltpu.SemaphoreType.DMA((COPIES,)),
    ]
    outs = pl.pallas_call(
        kernel,
        out_shape=(
            jax.ShapeDtypeStruct((ROWS, 256), BF16),
            jax.ShapeDtypeStruct((ROWS, 256), BF16),
            jax.ShapeDtypeStruct((ROWS, 256), BF16),
            jax.ShapeDtypeStruct((2, ROWS), F32),
            jax.ShapeDtypeStruct((16, ROWS), F32),
            jax.ShapeDtypeStruct((4, 1024), F32),
        ),
        in_specs=[vmem] * 7,
        out_specs=(vmem,) * 6,
        scratch_shapes=scratch,
        compiler_params=pltpu.CompilerParams(collective_id=0, has_side_effects=True),
    )(
        queries[0], key_vectors[0], value_vectors[0], out_cotangent[0],
        out_weight.reshape(256, 1024), log_decay[0], level_gates[0].reshape(16, ROWS),
    )
    qg, kg, vg, dg, gg, wg = outs
    return (
        qg[None], kg[None], vg[None], dg[None],
        gg.reshape(1, 2, 8, ROWS), wg.reshape(2, 2, 1024),
    )


def solution(mesh):
    placed = (
        P("dp", "ctx", "head"),
        P("dp", "ctx", "head"),
        P("dp", "ctx", "head"),
        P("dp", "ctx", None),
        P(None, "head", None),
        P("dp", "head", "ctx"),
        P("dp", "head", None, "ctx"),
    )
    return jax.shard_map(
        local,
        mesh=mesh,
        in_specs=placed,
        out_specs=(
            P("dp", "ctx", "head"),
            P("dp", "ctx", "head"),
            P("dp", "ctx", "head"),
            P("dp", "head", "ctx"),
            P("dp", "head", None, "ctx"),
            P(("dp", "ctx"), "head", None),
        ),
        check_vma=False,
    )
```

```python
import jax
import jax.numpy as jnp
from jax import lax
from jax.experimental import pallas as pl
from jax.experimental.pallas import tpu as pltpu
from jax.sharding import PartitionSpec as P

F32 = jnp.float32
BF16 = jnp.bfloat16
MESH = pl.DeviceIdType.MESH
NZ = 8
NY = 4
ROWS = 256
DH = 128
SPAN = 64
FAR = 5

NN = (((1,), (0,)), ((), ()))
NT = (((1,), (1,)), ((), ()))
TN = (((0,), (0,)), ((), ()))


def dot(a, b, dims):
    return lax.dot_general(a, b, dims, preferred_element_type=F32)


def iota(shape, dim):
    return lax.broadcasted_iota(jnp.int32, shape, dim)


def exact_dot(x, ones):
    hi = x.astype(BF16)
    rest = x - hi.astype(F32)
    mid = rest.astype(BF16)
    low = (rest - mid.astype(F32)).astype(BF16)
    return dot(hi, ones, NN) + dot(mid, ones, NN) + dot(low, ones, NN)


D_ROW = 0
D_COL = D_ROW + 8
F_ROW = D_COL + 4
F_COL = F_ROW + 8
S_UP = F_COL + 4
S_DOWN = S_UP + 8
T_UP = S_DOWN + 8
T_DOWN = T_UP + 4
Q_STEP = T_DOWN + 4
R_UP = Q_STEP + 10
R_DOWN = R_UP + 8
W_DP = R_DOWN + 8
W_Y = W_DP + 1
W_Z = W_Y + 6
COPIES = W_Z + 8


def kernel(
    q_ref, k_ref, v_ref, cot_ref, ow_ref, decay_ref, gates_ref,
    qg_ref, kg_ref, vg_ref, dg_ref, gg_ref, wg_ref,
    x_ref, xt_ref, zc_ref, zt_ref, flow_ref,
    dbuf, dcol, fbuf, fcol, etab, ctab,
    sbuf, tbuf, qs_ref, qa, qb, qc, qb2, qc2, pbuf, rsend, rrecv,
    g_ref, lifted_ref, lev_ref, attl_ref, qloc, kloc, vloc, att_ref,
    wbuf, wdp, usum, wa1, wb1, wa2, wb2, sa2, sb2, zsum, wz,
    ssem, rsem,
):
    ctx = lax.axis_index("ctx")
    dp = lax.axis_index("dp")
    y = lax.div(ctx, NZ)
    z = lax.rem(ctx, NZ)

    def zz(j):
        return lax.rem(z + j + NZ, NZ)

    def yy(j):
        return lax.rem(y + j + NY, NY)

    def at_z(j):
        return {"ctx": y * NZ + zz(j)}

    def at_y(j):
        return {"ctx": yy(j) * NZ + z}

    other = {"dp": 1 - dp}
    sent = []

    def copy(src, dst, n, where):
        return pltpu.make_async_remote_copy(
            src_ref=src, dst_ref=dst, send_sem=ssem.at[n], recv_sem=rsem.at[n],
            device_id=where, device_id_type=MESH,
        )

    def send(src, dst, n, where):
        c = copy(src, dst, n, where)
        c.start()
        sent.append(c)

    def arrived(dst, n, where):
        copy(dst, dst, n, where).wait_recv()

    barrier = pltpu.get_barrier_semaphore()
    for j in range(1, NZ):
        pl.semaphore_signal(barrier, inc=1, device_id=at_z(j), device_id_type=MESH)
    for j in range(1, NY):
        pl.semaphore_signal(barrier, inc=1, device_id=at_y(j), device_id_type=MESH)
    pl.semaphore_signal(barrier, inc=1, device_id=other, device_id_type=MESH)

    x_ref[...] = jnp.zeros_like(x_ref)
    x_ref[0:16, :] = gates_ref[...]
    x_ref[16:18, :] = decay_ref[...]
    upto = (iota((ROWS, ROWS), 0) <= iota((ROWS, ROWS), 1)).astype(BF16)
    cum = exact_dot(x_ref[16:24, :], upto)
    x_ref[24:32, :] = cum
    xt_ref[...] = jnp.transpose(x_ref[...])
    total = jnp.broadcast_to(cum[:, ROWS - 1 : ROWS], (8, 128))
    dbuf[pl.ds(z, 1)] = total[None]

    def cols(h):
        return slice(h * DH, (h + 1) * DH)

    def cum_col(h):
        return xt_ref[:, 24 + h : 25 + h]

    def to_end(h):
        return jnp.exp(x_ref[24 + h : 25 + h, ROWS - 1 : ROWS] - cum_col(h))

    def lift(h, m):
        return xt_ref[:, h * 8 + 3 + m : h * 8 + 4 + m] * jnp.exp(cum_col(h))

    for h in range(2):
        scaled = (to_end(h) * v_ref[:, cols(h)].astype(F32)).astype(BF16)
        sbuf[pl.ds(z, 1), h] = dot(k_ref[:, cols(h)], scaled, TN)[None]

    pl.semaphore_wait(barrier, NZ - 1 + NY - 1 + 1)

    for j in range(1, NZ):
        send(dbuf.at[z], dbuf.at[z], D_ROW + j, at_z(j))
    for h in range(2):
        send(sbuf.at[z, h], sbuf.at[z, h], S_UP + h, at_z(1))
        send(sbuf.at[z, h], sbuf.at[z, h], S_DOWN + h, at_z(-1))

    mixed = dot(cot_ref[...], ow_ref[...].reshape(256, 1024), NT).astype(BF16)
    ri, ci = iota((ROWS, ROWS), 0), iota((ROWS, ROWS), 1)
    perm = (ri == 2 * (ci & (DH - 1)) + jnp.right_shift(ci, 7)).astype(BF16)
    g_ref[...] = dot(mixed, perm, NN).astype(BF16)

    def make_qs(h):
        g = g_ref[:, cols(h)].astype(F32)
        for m in range(FAR):
            lifted_ref[h, :, m * DH : (m + 1) * DH] = (lift(h, m) * g).astype(BF16)
        allq = dot(q_ref[:, cols(h)], lifted_ref[h], TN)
        for m in range(FAR):
            qs_ref[h, m] = allq[:, m * DH : (m + 1) * DH]

    for h in range(2):
        make_qs(h)
        send(qs_ref.at[h, 4], qc.at[h], Q_STEP + h, at_y(-1))
        send(qs_ref.at[h, 4], qb.at[h], Q_STEP + 2 + h, at_y(1))
        send(qs_ref.at[h, 3], qa.at[h], Q_STEP + 4 + h, at_y(-1))

    for j in range(1, NZ):
        arrived(dbuf.at[zz(-j)], D_ROW + j, at_z(j))
    zero = jnp.zeros((8, 128), F32)
    running = zero
    before = []
    mine = zero
    for i in range(NZ):
        before.append(running)
        d = dbuf[i]
        mine = mine + jnp.where(i < z, d, zero)
        running = running + d
    row_total = running
    for i in range(NZ):
        after = before[i] + dbuf[i]
        etab[i] = jnp.exp(row_total - after)
        low = i < z
        ctab[i] = jnp.where(low, jnp.exp(jnp.where(low, mine - after, zero)), zero)
    dcol[pl.ds(y, 1), 0:8, :] = row_total[None]
    dcol[pl.ds(y, 1), 8:16, :] = mine[None]
    for j in range(1, NY):
        send(dcol.at[y], dcol.at[y], D_COL + j, at_y(j))

    def gather_step(k):
        for h in range(2):
            if k < 3 or h == 0:
                arrived(sbuf.at[zz(-k), h], S_UP + 2 * (k - 1) + h, at_z(1))
                send(sbuf.at[zz(-k), h], sbuf.at[zz(-k), h], S_UP + 2 * k + h, at_z(1))
            if k < 3 or h == 1:
                arrived(sbuf.at[zz(k), h], S_DOWN + 2 * (k - 1) + h, at_z(-1))
                send(sbuf.at[zz(k), h], sbuf.at[zz(k), h], S_DOWN + 2 * k + h, at_z(-1))

    def attend(h):
        q, k, v, g = q_ref[:, cols(h)], k_ref[:, cols(h)], v_ref[:, cols(h)], g_ref[:, cols(h)]
        rows, columns = iota((ROWS, ROWS), 0), iota((ROWS, ROWS), 1)
        causal = rows >= columns
        split = jnp.bitwise_xor(jnp.right_shift(rows, 6), jnp.right_shift(columns, 6))
        gap = cum_col(h) - x_ref[24 + h : 25 + h, :]
        decay = jnp.where(causal, jnp.exp(jnp.where(causal, gap, 0.0)), 0.0)
        gate = [xt_ref[:, h * 8 + l : h * 8 + l + 1] for l in range(3)]
        picked = jnp.where(split == 0, gate[0], jnp.where(split == 1, gate[1], gate[2]))
        mixing = picked * decay
        scores = dot(q, k, NT)
        gw = dot(g, v, NT)
        weights = (mixing * scores).astype(BF16)
        sg = gw * mixing
        sg_low = sg.astype(BF16)
        attl_ref[h] = dot(weights, v, NN)
        vloc[h] = dot(weights, g, TN)
        qloc[h] = dot(sg_low, k, NN)
        kloc[h] = dot(sg_low, q, TN)
        flow_ref[h : h + 1, :] = jnp.sum(sg * scores, 0, keepdims=True)
        plain = gw * scores * decay
        near = jnp.zeros((ROWS, 1), F32)
        for l in range(3):
            hit = (split == l) if l < 2 else (split >= 2)
            part = jnp.sum(jnp.where(hit, plain, 0.0), 1, keepdims=True)
            zc_ref[:, h * 8 + l : h * 8 + l + 1] = part
            near = near + gate[l] * part
        zc_ref[:, 16 + h : 17 + h] = near

    zc_ref[...] = jnp.zeros_like(zc_ref)
    flow_ref[...] = jnp.zeros_like(flow_ref)
    gather_step(1)
    attend(0)
    gather_step(2)
    for h in range(2):
        arrived(qc.at[h], Q_STEP + h, at_y(-1))
        send(qc.at[h], qc2.at[h], Q_STEP + 6 + h, at_y(-1))
        arrived(qb.at[h], Q_STEP + 2 + h, at_y(1))
        send(qb.at[h], qb2.at[h], Q_STEP + 8 + h, at_y(1))
    attend(1)
    gather_step(3)

    for j in range(1, NY):
        arrived(dcol.at[yy(-j)], D_COL + j, at_y(j))
    row1, row2 = dcol[1, 0:8, :], dcol[2, 0:8, :]
    w2, w3 = jnp.exp(dcol[2, 8:16, :]), jnp.exp(dcol[3, 8:16, :])
    wnext = jnp.exp(dcol[yy(1), 8:16, :])
    ca = jnp.where(lax.rem(y, 2) == 0, wnext, zero)
    cb = jnp.where(y == 0, w3 * jnp.exp(row1 + row2), zero)
    cb2 = jnp.where(y == 1, w3 * jnp.exp(row2), zero)
    cc = jnp.where(y == 1, w2, zero)
    cc2 = jnp.where(y == 0, w2 * jnp.exp(row1), zero)
    for h in range(2):
        arrived(qa.at[h], Q_STEP + 4 + h, at_y(-1))
        arrived(qc2.at[h], Q_STEP + 6 + h, at_y(-1))
        arrived(qb2.at[h], Q_STEP + 8 + h, at_y(1))
        s = slice(h, h + 1)
        pbuf[h] = (
            ca[s] * qa[h] + cb[s] * qb[h] + cb2[s] * qb2[h] + cc[s] * qc[h] + cc2[s] * qc2[h]
        )

    def contribution(h, target):
        e = etab[target, h : h + 1, :]
        c = ctab[target, h : h + 1, :]
        none = jnp.zeros_like(c)
        far = lax.div(target, 4) != lax.div(z, 4)
        same = lax.div(target, 2) == lax.div(z, 2)
        c3 = jnp.where(far, c, none)
        c1 = jnp.where(same, c, none)
        c2 = c - c3 - c1
        return e * pbuf[h] + c1 * qs_ref[h, 0] + c2 * qs_ref[h, 1] + c3 * qs_ref[h, 2]

    def reduce_step(k):
        for h in range(2):
            for up in (0, 1):
                first = 0 if h == 1 - up else 1
                if k < first:
                    continue
                sign = 1 if up else -1
                base = R_UP if up else R_DOWN
                mine_part = contribution(h, zz(sign * (4 - k)))
                if k > first:
                    arrived(rrecv.at[up, h, k - 1], base + 2 * (k - 1) + h, at_z(sign))
                    mine_part = mine_part + rrecv[up, h, k - 1]
                rsend[up, h, k] = mine_part
                send(rsend.at[up, h, k], rrecv.at[up, h, k], base + 2 * k + h, at_z(sign))

    reduce_step(0)

    for h in range(2):
        for k in range(1, 5):
            if k == 4:
                if h == 0:
                    arrived(sbuf.at[zz(-4), h], S_UP + 6 + h, at_z(1))
                else:
                    arrived(sbuf.at[zz(4), h], S_DOWN + 6 + h, at_z(-1))
                continue
            if k == 3:
                if h == 1:
                    arrived(sbuf.at[zz(-3), h], S_UP + 4 + h, at_z(1))
                else:
                    arrived(sbuf.at[zz(3), h], S_DOWN + 4 + h, at_z(-1))
        lev = [jnp.zeros((DH, DH), F32) for _ in range(3)]
        whole = jnp.zeros((DH, DH), F32)
        for i in range(NZ):
            s = sbuf[i, h]
            c = ctab[i, h : h + 1, :]
            none = jnp.zeros_like(c)
            far = lax.div(z, 4) != i // 4
            same = lax.div(z, 2) == i // 2
            c3 = jnp.where(far, c, none)
            c1 = jnp.where(same, c, none)
            c2 = c - c3 - c1
            lev[0] = lev[0] + c1 * s
            lev[1] = lev[1] + c2 * s
            lev[2] = lev[2] + c3 * s
            whole = whole + etab[i, h : h + 1, :] * s
        for m in range(3):
            lev_ref[h, :, m * DH : (m + 1) * DH] = lev[m].astype(BF16)
        tbuf[pl.ds(y, 1), h] = whole[None]
        send(tbuf.at[y, h], tbuf.at[y, h], T_UP + h, at_y(1))
        send(tbuf.at[y, h], tbuf.at[y, h], T_DOWN + h, at_y(-1))

    reduce_step(1)
    arrived(tbuf.at[yy(-1), 0], T_UP + 0, at_y(1))
    send(tbuf.at[yy(-1), 0], tbuf.at[yy(-1), 0], T_UP + 2, at_y(1))
    arrived(tbuf.at[yy(1), 1], T_DOWN + 1, at_y(-1))
    send(tbuf.at[yy(1), 1], tbuf.at[yy(1), 1], T_DOWN + 2, at_y(-1))
    arrived(tbuf.at[yy(-1), 1], T_UP + 1, at_y(1))
    arrived(tbuf.at[yy(1), 0], T_DOWN + 0, at_y(-1))
    reduce_step(2)
    arrived(tbuf.at[yy(-2), 0], T_UP + 2, at_y(1))
    arrived(tbuf.at[yy(2), 1], T_DOWN + 2, at_y(-1))

    f4 = jnp.where(lax.rem(y, 2) == 1, jnp.exp(mine), zero)
    f5 = jnp.where(y >= 2, jnp.exp(mine + jnp.where(y == 3, row2, zero)), zero)
    f5low = f5 * jnp.exp(row1)

    def far_rows(h):
        s = slice(h, h + 1)
        lev_ref[h, :, 3 * DH : 4 * DH] = (f4[s] * tbuf[yy(-1), h]).astype(BF16)
        lev_ref[h, :, 4 * DH : 5 * DH] = (f5[s] * tbuf[1, h] + f5low[s] * tbuf[0, h]).astype(BF16)
        projected = dot(q_ref[:, cols(h)], lev_ref[h], NN)
        g = g_ref[:, cols(h)].astype(F32)
        attended = attl_ref[h]
        extra = zc_ref[:, 16 + h : 17 + h]
        ecum = jnp.exp(cum_col(h))
        for m in range(FAR):
            part = projected[:, m * DH : (m + 1) * DH]
            coef = lift(h, m)
            attended = attended + coef * part
            inner = jnp.sum(part * g, 1, keepdims=True)
            zc_ref[:, h * 8 + 3 + m : h * 8 + 4 + m] = ecum * inner
            extra = extra + coef * inner
        zc_ref[:, 16 + h : 17 + h] = extra
        att_ref[:, cols(h)] = attended.astype(BF16)

    for h in range(2):
        far_rows(h)

    r, j = iota((512, ROWS), 0), iota((512, ROWS), 1)
    wanted = (r & 1) * DH + jnp.right_shift(r, 3) * 2 + (jnp.right_shift(r, 1) & 1)
    half = jnp.right_shift(r, 2) & 1
    match = wanted == j
    first_half = jnp.where(match & (half == 0), 1.0, 0.0).astype(BF16)
    second_half = jnp.where(match & (half == 1), 1.0, 0.0).astype(BF16)
    att = att_ref[...]
    lhs0 = dot(first_half, att, NT).astype(BF16)
    lhs1 = dot(second_half, att, NT).astype(BF16)
    wbuf[...] = dot(lhs0, cot_ref[:, 0:512], NN) + dot(lhs1, cot_ref[:, 512:1024], NN)
    theirs = pl.multiple_of((1 - dp) * 256, 256)
    ours = pl.multiple_of(dp * 256, 256)
    send(wbuf.at[pl.ds(theirs, 256)], wdp, W_DP, other)

    reduce_step(3)
    for h in range(2):
        qfar = dot(lifted_ref[h], lev_ref[h], NT)
        qg_ref[:, cols(h)] = (qloc[h] + qfar).astype(BF16)

    arrived(wdp, W_DP, other)
    usum[...] = wbuf[pl.ds(ours, 256), :] + wdp[...]

    def chunk(jy, start):
        return pl.ds(pl.multiple_of(yy(jy) * 64 + start, 32), 32)

    send(usum.at[chunk(2, 0)], wa1, W_Y + 0, at_y(1))
    send(usum.at[chunk(-2, 32)], wb1, W_Y + 1, at_y(-1))
    send(usum.at[chunk(1, 32)], wa2.at[pl.ds(32, 32)], W_Y + 2, at_y(1))
    send(usum.at[chunk(-1, 0)], wb2.at[pl.ds(0, 32)], W_Y + 3, at_y(-1))

    zt_ref[...] = jnp.transpose(zc_ref[...])
    gg_ref[...] = zt_ref[0:16, :]
    for h in range(2):
        arrived(rrecv.at[1, h, 3], R_UP + 6 + h, at_z(1))
        arrived(rrecv.at[0, h, 3], R_DOWN + 6 + h, at_z(-1))
        e = etab[z, h : h + 1, :]
        returned = (e * pbuf[h] + rrecv[1, h, 3] + rrecv[0, h, 3]).astype(BF16)
        k, v = k_ref[:, cols(h)], v_ref[:, cols(h)]
        w = to_end(h)
        kfar = w * dot(v, returned, NT)
        vfar = w * dot(k, returned, NN)
        kg_ref[:, cols(h)] = (kloc[h] + kfar).astype(BF16)
        vg_ref[:, cols(h)] = (vloc[h] + vfar).astype(BF16)
        zc_ref[:, 24 + h : 25 + h] = jnp.sum(k.astype(F32) * kfar, 1, keepdims=True)

    arrived(wa1, W_Y + 0, at_y(1))
    sa2[...] = usum[chunk(1, 0), :] + wa1[...]
    send(sa2, wa2.at[pl.ds(0, 32)], W_Y + 4, at_y(1))
    arrived(wb1, W_Y + 1, at_y(-1))
    sb2[...] = usum[chunk(-1, 32), :] + wb1[...]
    send(sb2, wb2.at[pl.ds(32, 32)], W_Y + 5, at_y(-1))

    back = jnp.transpose(zc_ref[...])
    flow = zt_ref[16:24, :] - flow_ref[...] - back[24:32, :]
    block_flow = jnp.broadcast_to(jnp.sum(flow, 1, keepdims=True), (8, 128))
    fbuf[pl.ds(z, 1)] = block_flow[None]
    for jz in range(1, NZ):
        send(fbuf.at[z], fbuf.at[z], F_ROW + jz, at_z(jz))
    onward = (iota((ROWS, ROWS), 0) >= iota((ROWS, ROWS), 1)).astype(BF16)
    within = exact_dot(flow, onward)

    arrived(wa2.at[pl.ds(32, 32)], W_Y + 2, at_y(1))
    arrived(wb2.at[pl.ds(0, 32)], W_Y + 3, at_y(-1))
    arrived(wa2.at[pl.ds(0, 32)], W_Y + 4, at_y(1))
    arrived(wb2.at[pl.ds(32, 32)], W_Y + 5, at_y(-1))
    own = pl.ds(pl.multiple_of(y * 64, 64), 64)
    zsum[...] = usum[own, :] + wa2[...] + wb2[...]

    def part_of(jz):
        return pl.ds(pl.multiple_of(zz(jz) * 8, 8), 8)

    for jz in range(1, NZ):
        send(zsum.at[part_of(jz)], wz.at[jz], W_Z + jz, at_z(jz))

    tail = zero
    row_flow = zero
    for jz in range(1, NZ):
        arrived(fbuf.at[zz(-jz)], F_ROW + jz, at_z(jz))
    for i in range(NZ):
        f = fbuf[i]
        row_flow = row_flow + f
        tail = tail + jnp.where(i > z, f, zero)
    fcol[pl.ds(y, 1)] = row_flow[None]
    for jy in range(1, NY):
        send(fcol.at[y], fcol.at[y], F_COL + jy, at_y(jy))

    result = zsum[part_of(0), :]
    for jz in range(1, NZ):
        arrived(wz.at[jz], W_Z + jz, at_z(jz))
        result = result + wz[jz]
    for i in range(2):
        wg_ref[i, :, 0:512] = result[2 * i : 2 * i + 2, :]
        wg_ref[i, :, 512:1024] = result[4 + 2 * i : 6 + 2 * i, :]

    for jy in range(1, NY):
        arrived(fcol.at[yy(-jy)], F_COL + jy, at_y(jy))
    for i in range(NY):
        tail = tail + jnp.where(i > y, fcol[i], zero)
    dg_ref[...] = (within + tail[:, 0:1])[0:2, :]

    for c in sent:
        c.wait_send()


def hand_over(*refs):
    for i in range(6):
        refs[6 + i][...] = refs[i][...]


def local(queries, key_vectors, value_vectors, out_cotangent, out_weight, log_decay, level_gates):
    v32 = lambda *s: pltpu.VMEM(s, F32)
    v16 = lambda *s: pltpu.VMEM(s, BF16)
    vmem = pl.BlockSpec(memory_space=pltpu.VMEM)
    scratch = [
        v32(128, ROWS), v32(ROWS, 128), v32(ROWS, 128), v32(128, ROWS), v32(8, ROWS),
        v32(NZ, 8, 128), v32(NY, 16, 128), v32(NZ, 8, 128), v32(NY, 8, 128),
        v32(NZ, 8, 128), v32(NZ, 8, 128),
        v32(NZ, 2, DH, DH), v32(NY, 2, DH, DH), v32(2, FAR, DH, DH),
        v32(2, DH, DH), v32(2, DH, DH), v32(2, DH, DH), v32(2, DH, DH), v32(2, DH, DH),
        v32(2, DH, DH), v32(2, 2, 4, DH, DH), v32(2, 2, 4, DH, DH),
        v16(ROWS, 256), v16(2, ROWS, FAR * DH), v16(2, DH, FAR * DH), v32(2, ROWS, DH),
        v32(2, ROWS, DH), v32(2, ROWS, DH), v32(2, ROWS, DH), v16(ROWS, 256),
        v32(512, 512), v32(256, 512), v32(256, 512), v32(32, 512), v32(32, 512),
        v32(64, 512), v32(64, 512), v32(32, 512), v32(32, 512), v32(64, 512), v32(NZ, 8, 512),
        pltpu.SemaphoreType.DMA((COPIES,)), pltpu.SemaphoreType.DMA((COPIES,)),
    ]
    outs = pl.pallas_call(
        kernel,
        out_shape=(
            jax.ShapeDtypeStruct((ROWS, 256), BF16),
            jax.ShapeDtypeStruct((ROWS, 256), BF16),
            jax.ShapeDtypeStruct((ROWS, 256), BF16),
            jax.ShapeDtypeStruct((2, ROWS), F32),
            jax.ShapeDtypeStruct((16, ROWS), F32),
            jax.ShapeDtypeStruct((2, 2, 1024), F32),
        ),
        in_specs=[vmem] * 7,
        out_specs=(vmem,) * 6,
        scratch_shapes=scratch,
        compiler_params=pltpu.CompilerParams(collective_id=0, has_side_effects=True),
    )(
        queries[0], key_vectors[0], value_vectors[0], out_cotangent[0],
        out_weight, log_decay[0], level_gates[0].reshape(16, ROWS),
    )
    qg, kg, vg, dg, gg, wg = pl.pallas_call(
        hand_over,
        out_shape=tuple(jax.ShapeDtypeStruct(o.shape, o.dtype) for o in outs),
        in_specs=[vmem] * 6,
        out_specs=(vmem,) * 6,
    )(*outs)
    return (
        qg[None], kg[None], vg[None], dg[None],
        gg.reshape(1, 2, 8, ROWS), wg,
    )


def solution(mesh):
    placed = (
        P("dp", "ctx", "head"),
        P("dp", "ctx", "head"),
        P("dp", "ctx", "head"),
        P("dp", "ctx", None),
        P(None, "head", None),
        P("dp", "head", "ctx"),
        P("dp", "head", None, "ctx"),
    )
    return jax.shard_map(
        local,
        mesh=mesh,
        in_specs=placed,
        out_specs=(
            P("dp", "ctx", "head"),
            P("dp", "ctx", "head"),
            P("dp", "ctx", "head"),
            P("dp", "head", "ctx"),
            P("dp", "head", None, "ctx"),
            P(("dp", "ctx"), "head", None),
        ),
        check_vma=False,
    )
```

```python
import jax
import jax.numpy as jnp
from jax import lax
from jax.experimental import pallas as pl
from jax.experimental.pallas import tpu as pltpu
from jax.sharding import PartitionSpec as P

F32 = jnp.float32
BF16 = jnp.bfloat16
MESH = pl.DeviceIdType.MESH
NZ = 8
NY = 4
ROWS = 256
DH = 128
SPAN = 64
FAR = 5

NN = (((1,), (0,)), ((), ()))
NT = (((1,), (1,)), ((), ()))
TN = (((0,), (0,)), ((), ()))


def dot(a, b, dims):
    return lax.dot_general(a, b, dims, preferred_element_type=F32)


def iota(shape, dim):
    return lax.broadcasted_iota(jnp.int32, shape, dim)


def exact_dot(x, ones):
    hi = x.astype(BF16)
    rest = x - hi.astype(F32)
    mid = rest.astype(BF16)
    low = (rest - mid.astype(F32)).astype(BF16)
    return dot(hi, ones, NN) + dot(mid, ones, NN) + dot(low, ones, NN)


D_ROW = 0
D_COL = D_ROW + 8
F_ROW = D_COL + 4
F_COL = F_ROW + 8
S_UP = F_COL + 4
S_DOWN = S_UP + 8
T_UP = S_DOWN + 8
T_DOWN = T_UP + 4
Q_STEP = T_DOWN + 4
R_UP = Q_STEP + 10
R_DOWN = R_UP + 8
W_DP = R_DOWN + 8
W_Y = W_DP + 1
W_Z = W_Y + 6
COPIES = W_Z + 8


def kernel(
    q_ref, k_ref, v_ref, cot_ref, ow_ref, decay_ref, gates_ref,
    qg_ref, kg_ref, vg_ref, dg_ref, gg_ref, wg_ref,
    x_ref, xt_ref, zc_ref, zt_ref, flow_ref,
    dbuf, dcol, fbuf, fcol, etab, ctab,
    sbuf, tbuf, qs_ref, qa, qb, qc, qb2, qc2, pbuf, rsend, rrecv,
    g_ref, lifted_ref, lev_ref, attl_ref, qloc, kloc, vloc, att_ref,
    wbuf, wdp, usum, wa1, wb1, wa2, wb2, sa2, sb2, zsum, wz,
    ssem, rsem,
):
    ctx = lax.axis_index("ctx")
    dp = lax.axis_index("dp")
    y = lax.div(ctx, NZ)
    z = lax.rem(ctx, NZ)

    def zz(j):
        return lax.rem(z + j + NZ, NZ)

    def yy(j):
        return lax.rem(y + j + NY, NY)

    def at_z(j):
        return {"ctx": y * NZ + zz(j)}

    def at_y(j):
        return {"ctx": yy(j) * NZ + z}

    other = {"dp": 1 - dp}
    sent = []

    def copy(src, dst, n, where):
        return pltpu.make_async_remote_copy(
            src_ref=src, dst_ref=dst, send_sem=ssem.at[n], recv_sem=rsem.at[n],
            device_id=where, device_id_type=MESH,
        )

    def send(src, dst, n, where):
        c = copy(src, dst, n, where)
        c.start()
        sent.append(c)

    def arrived(dst, n, where):
        copy(dst, dst, n, where).wait_recv()

    barrier = pltpu.get_barrier_semaphore()
    for j in range(1, NZ):
        pl.semaphore_signal(barrier, inc=1, device_id=at_z(j), device_id_type=MESH)
    for j in range(1, NY):
        pl.semaphore_signal(barrier, inc=1, device_id=at_y(j), device_id_type=MESH)
    pl.semaphore_signal(barrier, inc=1, device_id=other, device_id_type=MESH)

    x_ref[...] = jnp.zeros_like(x_ref)
    x_ref[0:16, :] = gates_ref[...]
    x_ref[16:18, :] = decay_ref[...]
    upto = (iota((ROWS, ROWS), 0) <= iota((ROWS, ROWS), 1)).astype(BF16)
    cum = exact_dot(x_ref[16:24, :], upto)
    x_ref[24:32, :] = cum
    xt_ref[...] = jnp.transpose(x_ref[...])
    total = jnp.broadcast_to(cum[:, ROWS - 1 : ROWS], (8, 128))
    dbuf[pl.ds(z, 1)] = total[None]

    def cols(h):
        return slice(h * DH, (h + 1) * DH)

    def cum_col(h):
        return xt_ref[:, 24 + h : 25 + h]

    def to_end(h):
        return jnp.exp(x_ref[24 + h : 25 + h, ROWS - 1 : ROWS] - cum_col(h))

    def lift(h, m):
        return xt_ref[:, h * 8 + 3 + m : h * 8 + 4 + m] * jnp.exp(cum_col(h))

    for h in range(2):
        scaled = (to_end(h) * v_ref[:, cols(h)].astype(F32)).astype(BF16)
        sbuf[pl.ds(z, 1), h] = dot(k_ref[:, cols(h)], scaled, TN)[None]

    pl.semaphore_wait(barrier, NZ - 1 + NY - 1 + 1)

    for j in range(1, NZ):
        send(dbuf.at[z], dbuf.at[z], D_ROW + j, at_z(j))
    for h in range(2):
        send(sbuf.at[z, h], sbuf.at[z, h], S_UP + h, at_z(1))
        send(sbuf.at[z, h], sbuf.at[z, h], S_DOWN + h, at_z(-1))

    mixed = dot(cot_ref[...], ow_ref[...].reshape(256, 1024), NT).astype(BF16)
    ri, ci = iota((ROWS, ROWS), 0), iota((ROWS, ROWS), 1)
    perm = (ri == 2 * (ci & (DH - 1)) + jnp.right_shift(ci, 7)).astype(BF16)
    g_ref[...] = dot(mixed, perm, NN).astype(BF16)

    def make_qs(h):
        g = g_ref[:, cols(h)].astype(F32)
        for m in range(FAR):
            lifted_ref[h, :, m * DH : (m + 1) * DH] = (lift(h, m) * g).astype(BF16)
        allq = dot(q_ref[:, cols(h)], lifted_ref[h], TN)
        for m in range(FAR):
            qs_ref[h, m] = allq[:, m * DH : (m + 1) * DH]

    for h in range(2):
        make_qs(h)
        send(qs_ref.at[h, 4], qc.at[h], Q_STEP + h, at_y(-1))
        send(qs_ref.at[h, 4], qb.at[h], Q_STEP + 2 + h, at_y(1))
        send(qs_ref.at[h, 3], qa.at[h], Q_STEP + 4 + h, at_y(-1))

    for j in range(1, NZ):
        arrived(dbuf.at[zz(-j)], D_ROW + j, at_z(j))
    zero = jnp.zeros((8, 128), F32)
    running = zero
    before = []
    mine = zero
    for i in range(NZ):
        before.append(running)
        d = dbuf[i]
        mine = mine + jnp.where(i < z, d, zero)
        running = running + d
    row_total = running
    for i in range(NZ):
        after = before[i] + dbuf[i]
        etab[i] = jnp.exp(row_total - after)
        low = i < z
        ctab[i] = jnp.where(low, jnp.exp(jnp.where(low, mine - after, zero)), zero)
    dcol[pl.ds(y, 1), 0:8, :] = row_total[None]
    dcol[pl.ds(y, 1), 8:16, :] = mine[None]
    for j in range(1, NY):
        send(dcol.at[y], dcol.at[y], D_COL + j, at_y(j))

    def gather_step(k):
        for h in range(2):
            if k < 3 or h == 0:
                arrived(sbuf.at[zz(-k), h], S_UP + 2 * (k - 1) + h, at_z(1))
                send(sbuf.at[zz(-k), h], sbuf.at[zz(-k), h], S_UP + 2 * k + h, at_z(1))
            if k < 3 or h == 1:
                arrived(sbuf.at[zz(k), h], S_DOWN + 2 * (k - 1) + h, at_z(-1))
                send(sbuf.at[zz(k), h], sbuf.at[zz(k), h], S_DOWN + 2 * k + h, at_z(-1))

    def attend(h):
        q, k, v, g = q_ref[:, cols(h)], k_ref[:, cols(h)], v_ref[:, cols(h)], g_ref[:, cols(h)]
        rows, columns = iota((ROWS, ROWS), 0), iota((ROWS, ROWS), 1)
        causal = rows >= columns
        split = jnp.bitwise_xor(jnp.right_shift(rows, 6), jnp.right_shift(columns, 6))
        gap = cum_col(h) - x_ref[24 + h : 25 + h, :]
        decay = jnp.where(causal, jnp.exp(jnp.where(causal, gap, 0.0)), 0.0)
        gate = [xt_ref[:, h * 8 + l : h * 8 + l + 1] for l in range(3)]
        picked = jnp.where(split == 0, gate[0], jnp.where(split == 1, gate[1], gate[2]))
        mixing = picked * decay
        scores = dot(q, k, NT)
        gw = dot(g, v, NT)
        weights = (mixing * scores).astype(BF16)
        sg = gw * mixing
        sg_low = sg.astype(BF16)
        attl_ref[h] = dot(weights, v, NN)
        vloc[h] = dot(weights, g, TN)
        qloc[h] = dot(sg_low, k, NN)
        kloc[h] = dot(sg_low, q, TN)
        flow_ref[h : h + 1, :] = jnp.sum(sg * scores, 0, keepdims=True)
        plain = gw * scores * decay
        near = jnp.zeros((ROWS, 1), F32)
        for l in range(3):
            hit = (split == l) if l < 2 else (split >= 2)
            part = jnp.sum(jnp.where(hit, plain, 0.0), 1, keepdims=True)
            zc_ref[:, h * 8 + l : h * 8 + l + 1] = part
            near = near + gate[l] * part
        zc_ref[:, 16 + h : 17 + h] = near

    zc_ref[...] = jnp.zeros_like(zc_ref)
    flow_ref[...] = jnp.zeros_like(flow_ref)
    gather_step(1)
    attend(0)
    gather_step(2)
    for h in range(2):
        arrived(qc.at[h], Q_STEP + h, at_y(-1))
        send(qc.at[h], qc2.at[h], Q_STEP + 6 + h, at_y(-1))
        arrived(qb.at[h], Q_STEP + 2 + h, at_y(1))
        send(qb.at[h], qb2.at[h], Q_STEP + 8 + h, at_y(1))
    attend(1)
    gather_step(3)

    for j in range(1, NY):
        arrived(dcol.at[yy(-j)], D_COL + j, at_y(j))
    row1, row2 = dcol[1, 0:8, :], dcol[2, 0:8, :]
    w2, w3 = jnp.exp(dcol[2, 8:16, :]), jnp.exp(dcol[3, 8:16, :])
    wnext = jnp.exp(dcol[yy(1), 8:16, :])
    ca = jnp.where(lax.rem(y, 2) == 0, wnext, zero)
    cb = jnp.where(y == 0, w3 * jnp.exp(row1 + row2), zero)
    cb2 = jnp.where(y == 1, w3 * jnp.exp(row2), zero)
    cc = jnp.where(y == 1, w2, zero)
    cc2 = jnp.where(y == 0, w2 * jnp.exp(row1), zero)
    for h in range(2):
        arrived(qa.at[h], Q_STEP + 4 + h, at_y(-1))
        arrived(qc2.at[h], Q_STEP + 6 + h, at_y(-1))
        arrived(qb2.at[h], Q_STEP + 8 + h, at_y(1))
        s = slice(h, h + 1)
        pbuf[h] = (
            ca[s] * qa[h] + cb[s] * qb[h] + cb2[s] * qb2[h] + cc[s] * qc[h] + cc2[s] * qc2[h]
        )

    def contribution(h, target):
        e = etab[target, h : h + 1, :]
        c = ctab[target, h : h + 1, :]
        none = jnp.zeros_like(c)
        far = lax.div(target, 4) != lax.div(z, 4)
        same = lax.div(target, 2) == lax.div(z, 2)
        c3 = jnp.where(far, c, none)
        c1 = jnp.where(same, c, none)
        c2 = c - c3 - c1
        return e * pbuf[h] + c1 * qs_ref[h, 0] + c2 * qs_ref[h, 1] + c3 * qs_ref[h, 2]

    def reduce_step(k):
        for h in range(2):
            for up in (0, 1):
                first = 0 if h == 1 - up else 1
                if k < first:
                    continue
                sign = 1 if up else -1
                base = R_UP if up else R_DOWN
                mine_part = contribution(h, zz(sign * (4 - k)))
                if k > first:
                    arrived(rrecv.at[up, h, k - 1], base + 2 * (k - 1) + h, at_z(sign))
                    mine_part = mine_part + rrecv[up, h, k - 1]
                rsend[up, h, k] = mine_part
                send(rsend.at[up, h, k], rrecv.at[up, h, k], base + 2 * k + h, at_z(sign))

    reduce_step(0)

    for h in range(2):
        for k in range(1, 5):
            if k == 4:
                if h == 0:
                    arrived(sbuf.at[zz(-4), h], S_UP + 6 + h, at_z(1))
                else:
                    arrived(sbuf.at[zz(4), h], S_DOWN + 6 + h, at_z(-1))
                continue
            if k == 3:
                if h == 1:
                    arrived(sbuf.at[zz(-3), h], S_UP + 4 + h, at_z(1))
                else:
                    arrived(sbuf.at[zz(3), h], S_DOWN + 4 + h, at_z(-1))
        lev = [jnp.zeros((DH, DH), F32) for _ in range(3)]
        whole = jnp.zeros((DH, DH), F32)
        for i in range(NZ):
            s = sbuf[i, h]
            c = ctab[i, h : h + 1, :]
            none = jnp.zeros_like(c)
            far = lax.div(z, 4) != i // 4
            same = lax.div(z, 2) == i // 2
            c3 = jnp.where(far, c, none)
            c1 = jnp.where(same, c, none)
            c2 = c - c3 - c1
            lev[0] = lev[0] + c1 * s
            lev[1] = lev[1] + c2 * s
            lev[2] = lev[2] + c3 * s
            whole = whole + etab[i, h : h + 1, :] * s
        for m in range(3):
            lev_ref[h, :, m * DH : (m + 1) * DH] = lev[m].astype(BF16)
        tbuf[pl.ds(y, 1), h] = whole[None]
        send(tbuf.at[y, h], tbuf.at[y, h], T_UP + h, at_y(1))
        send(tbuf.at[y, h], tbuf.at[y, h], T_DOWN + h, at_y(-1))

    reduce_step(1)
    arrived(tbuf.at[yy(-1), 0], T_UP + 0, at_y(1))
    send(tbuf.at[yy(-1), 0], tbuf.at[yy(-1), 0], T_UP + 2, at_y(1))
    arrived(tbuf.at[yy(1), 1], T_DOWN + 1, at_y(-1))
    send(tbuf.at[yy(1), 1], tbuf.at[yy(1), 1], T_DOWN + 2, at_y(-1))
    arrived(tbuf.at[yy(-1), 1], T_UP + 1, at_y(1))
    arrived(tbuf.at[yy(1), 0], T_DOWN + 0, at_y(-1))
    reduce_step(2)
    arrived(tbuf.at[yy(-2), 0], T_UP + 2, at_y(1))
    arrived(tbuf.at[yy(2), 1], T_DOWN + 2, at_y(-1))

    f4 = jnp.where(lax.rem(y, 2) == 1, jnp.exp(mine), zero)
    f5 = jnp.where(y >= 2, jnp.exp(mine + jnp.where(y == 3, row2, zero)), zero)
    f5low = f5 * jnp.exp(row1)

    def far_rows(h):
        s = slice(h, h + 1)
        lev_ref[h, :, 3 * DH : 4 * DH] = (f4[s] * tbuf[yy(-1), h]).astype(BF16)
        lev_ref[h, :, 4 * DH : 5 * DH] = (f5[s] * tbuf[1, h] + f5low[s] * tbuf[0, h]).astype(BF16)
        projected = dot(q_ref[:, cols(h)], lev_ref[h], NN)
        g = g_ref[:, cols(h)].astype(F32)
        attended = attl_ref[h]
        extra = zc_ref[:, 16 + h : 17 + h]
        ecum = jnp.exp(cum_col(h))
        for m in range(FAR):
            part = projected[:, m * DH : (m + 1) * DH]
            coef = lift(h, m)
            attended = attended + coef * part
            inner = jnp.sum(part * g, 1, keepdims=True)
            zc_ref[:, h * 8 + 3 + m : h * 8 + 4 + m] = ecum * inner
            extra = extra + coef * inner
        zc_ref[:, 16 + h : 17 + h] = extra
        att_ref[:, cols(h)] = attended.astype(BF16)

    for h in range(2):
        far_rows(h)

    r, j = iota((512, ROWS), 0), iota((512, ROWS), 1)
    wanted = (r & 1) * DH + jnp.right_shift(r, 3) * 2 + (jnp.right_shift(r, 1) & 1)
    half = jnp.right_shift(r, 2) & 1
    match = wanted == j
    first_half = jnp.where(match & (half == 0), 1.0, 0.0).astype(BF16)
    second_half = jnp.where(match & (half == 1), 1.0, 0.0).astype(BF16)
    att = att_ref[...]
    lhs0 = dot(first_half, att, NT).astype(BF16)
    lhs1 = dot(second_half, att, NT).astype(BF16)
    wbuf[...] = dot(lhs0, cot_ref[:, 0:512], NN) + dot(lhs1, cot_ref[:, 512:1024], NN)
    theirs = pl.multiple_of((1 - dp) * 256, 256)
    ours = pl.multiple_of(dp * 256, 256)
    send(wbuf.at[pl.ds(theirs, 256)], wdp, W_DP, other)

    reduce_step(3)
    for h in range(2):
        qfar = dot(lifted_ref[h], lev_ref[h], NT)
        qg_ref[:, cols(h)] = (qloc[h] + qfar).astype(BF16)

    arrived(wdp, W_DP, other)
    usum[...] = wbuf[pl.ds(ours, 256), :] + wdp[...]

    def chunk(jy, start):
        return pl.ds(pl.multiple_of(yy(jy) * 64 + start, 32), 32)

    send(usum.at[chunk(2, 0)], wa1, W_Y + 0, at_y(1))
    send(usum.at[chunk(-2, 32)], wb1, W_Y + 1, at_y(-1))
    send(usum.at[chunk(1, 32)], wa2.at[pl.ds(32, 32)], W_Y + 2, at_y(1))
    send(usum.at[chunk(-1, 0)], wb2.at[pl.ds(0, 32)], W_Y + 3, at_y(-1))

    zt_ref[...] = jnp.transpose(zc_ref[...])
    gg_ref[...] = zt_ref[0:16, :]
    for h in range(2):
        arrived(rrecv.at[1, h, 3], R_UP + 6 + h, at_z(1))
        arrived(rrecv.at[0, h, 3], R_DOWN + 6 + h, at_z(-1))
        e = etab[z, h : h + 1, :]
        returned = (e * pbuf[h] + rrecv[1, h, 3] + rrecv[0, h, 3]).astype(BF16)
        k, v = k_ref[:, cols(h)], v_ref[:, cols(h)]
        w = to_end(h)
        kfar = w * dot(v, returned, NT)
        vfar = w * dot(k, returned, NN)
        kg_ref[:, cols(h)] = (kloc[h] + kfar).astype(BF16)
        vg_ref[:, cols(h)] = (vloc[h] + vfar).astype(BF16)
        zc_ref[:, 24 + h : 25 + h] = jnp.sum(k.astype(F32) * kfar, 1, keepdims=True)

    arrived(wa1, W_Y + 0, at_y(1))
    sa2[...] = usum[chunk(1, 0), :] + wa1[...]
    send(sa2, wa2.at[pl.ds(0, 32)], W_Y + 4, at_y(1))
    arrived(wb1, W_Y + 1, at_y(-1))
    sb2[...] = usum[chunk(-1, 32), :] + wb1[...]
    send(sb2, wb2.at[pl.ds(32, 32)], W_Y + 5, at_y(-1))

    back = jnp.transpose(zc_ref[...])
    flow = zt_ref[16:24, :] - flow_ref[...] - back[24:32, :]
    block_flow = jnp.broadcast_to(jnp.sum(flow, 1, keepdims=True), (8, 128))
    fbuf[pl.ds(z, 1)] = block_flow[None]
    for jz in range(1, NZ):
        send(fbuf.at[z], fbuf.at[z], F_ROW + jz, at_z(jz))
    onward = (iota((ROWS, ROWS), 0) >= iota((ROWS, ROWS), 1)).astype(BF16)
    within = exact_dot(flow, onward)

    arrived(wa2.at[pl.ds(32, 32)], W_Y + 2, at_y(1))
    arrived(wb2.at[pl.ds(0, 32)], W_Y + 3, at_y(-1))
    arrived(wa2.at[pl.ds(0, 32)], W_Y + 4, at_y(1))
    arrived(wb2.at[pl.ds(32, 32)], W_Y + 5, at_y(-1))
    own = pl.ds(pl.multiple_of(y * 64, 64), 64)
    zsum[...] = usum[own, :] + wa2[...] + wb2[...]

    def part_of(jz):
        return pl.ds(pl.multiple_of(zz(jz) * 8, 8), 8)

    for jz in (4, 3, 5, 2, 6, 1, 7):
        send(zsum.at[part_of(jz)], wz.at[jz], W_Z + jz, at_z(jz))

    tail = zero
    row_flow = zero
    for jz in range(1, NZ):
        arrived(fbuf.at[zz(-jz)], F_ROW + jz, at_z(jz))
    for i in range(NZ):
        f = fbuf[i]
        row_flow = row_flow + f
        tail = tail + jnp.where(i > z, f, zero)
    fcol[pl.ds(y, 1)] = row_flow[None]
    for jy in range(1, NY):
        send(fcol.at[y], fcol.at[y], F_COL + jy, at_y(jy))

    result = zsum[part_of(0), :]
    for jz in range(1, NZ):
        arrived(wz.at[jz], W_Z + jz, at_z(jz))
        result = result + wz[jz]
    for i in range(2):
        wg_ref[i, :, 0:512] = result[2 * i : 2 * i + 2, :]
        wg_ref[i, :, 512:1024] = result[4 + 2 * i : 6 + 2 * i, :]

    for jy in range(1, NY):
        arrived(fcol.at[yy(-jy)], F_COL + jy, at_y(jy))
    for i in range(NY):
        tail = tail + jnp.where(i > y, fcol[i], zero)
    dg_ref[...] = (within + tail[:, 0:1])[0:2, :]

    for c in sent:
        c.wait_send()


def hand_over(*refs):
    for i in range(6):
        refs[6 + i][...] = refs[i][...]


def local(queries, key_vectors, value_vectors, out_cotangent, out_weight, log_decay, level_gates):
    v32 = lambda *s: pltpu.VMEM(s, F32)
    v16 = lambda *s: pltpu.VMEM(s, BF16)
    vmem = pl.BlockSpec(memory_space=pltpu.VMEM)
    scratch = [
        v32(128, ROWS), v32(ROWS, 128), v32(ROWS, 128), v32(128, ROWS), v32(8, ROWS),
        v32(NZ, 8, 128), v32(NY, 16, 128), v32(NZ, 8, 128), v32(NY, 8, 128),
        v32(NZ, 8, 128), v32(NZ, 8, 128),
        v32(NZ, 2, DH, DH), v32(NY, 2, DH, DH), v32(2, FAR, DH, DH),
        v32(2, DH, DH), v32(2, DH, DH), v32(2, DH, DH), v32(2, DH, DH), v32(2, DH, DH),
        v32(2, DH, DH), v32(2, 2, 4, DH, DH), v32(2, 2, 4, DH, DH),
        v16(ROWS, 256), v16(2, ROWS, FAR * DH), v16(2, DH, FAR * DH), v32(2, ROWS, DH),
        v32(2, ROWS, DH), v32(2, ROWS, DH), v32(2, ROWS, DH), v16(ROWS, 256),
        v32(512, 512), v32(256, 512), v32(256, 512), v32(32, 512), v32(32, 512),
        v32(64, 512), v32(64, 512), v32(32, 512), v32(32, 512), v32(64, 512), v32(NZ, 8, 512),
        pltpu.SemaphoreType.DMA((COPIES,)), pltpu.SemaphoreType.DMA((COPIES,)),
    ]
    outs = pl.pallas_call(
        kernel,
        out_shape=(
            jax.ShapeDtypeStruct((ROWS, 256), BF16),
            jax.ShapeDtypeStruct((ROWS, 256), BF16),
            jax.ShapeDtypeStruct((ROWS, 256), BF16),
            jax.ShapeDtypeStruct((2, ROWS), F32),
            jax.ShapeDtypeStruct((16, ROWS), F32),
            jax.ShapeDtypeStruct((2, 2, 1024), F32),
        ),
        in_specs=[vmem] * 7,
        out_specs=(vmem,) * 6,
        scratch_shapes=scratch,
        compiler_params=pltpu.CompilerParams(collective_id=0, has_side_effects=True),
    )(
        queries[0], key_vectors[0], value_vectors[0], out_cotangent[0],
        out_weight, log_decay[0], level_gates[0].reshape(16, ROWS),
    )
    qg, kg, vg, dg, gg, wg = pl.pallas_call(
        hand_over,
        out_shape=tuple(jax.ShapeDtypeStruct(o.shape, o.dtype) for o in outs),
        in_specs=[vmem] * 6,
        out_specs=(vmem,) * 6,
    )(*outs)
    return (
        qg[None], kg[None], vg[None], dg[None],
        gg.reshape(1, 2, 8, ROWS), wg,
    )


def solution(mesh):
    placed = (
        P("dp", "ctx", "head"),
        P("dp", "ctx", "head"),
        P("dp", "ctx", "head"),
        P("dp", "ctx", None),
        P(None, "head", None),
        P("dp", "head", "ctx"),
        P("dp", "head", None, "ctx"),
    )
    return jax.shard_map(
        local,
        mesh=mesh,
        in_specs=placed,
        out_specs=(
            P("dp", "ctx", "head"),
            P("dp", "ctx", "head"),
            P("dp", "ctx", "head"),
            P("dp", "head", "ctx"),
            P("dp", "head", None, "ctx"),
            P(("dp", "ctx"), "head", None),
        ),
        check_vma=False,
    )
```

```python
import jax
import jax.numpy as jnp
from jax import lax
from jax.experimental import pallas as pl
from jax.experimental.pallas import tpu as pltpu
from jax.sharding import PartitionSpec as P

F32 = jnp.float32
BF16 = jnp.bfloat16
MESH = pl.DeviceIdType.MESH
NZ = 8
NY = 4
ROWS = 256
DH = 128
SPAN = 64
FAR = 5

NN = (((1,), (0,)), ((), ()))
NT = (((1,), (1,)), ((), ()))
TN = (((0,), (0,)), ((), ()))


def dot(a, b, dims):
    return lax.dot_general(a, b, dims, preferred_element_type=F32)


def iota(shape, dim):
    return lax.broadcasted_iota(jnp.int32, shape, dim)


def exact_dot(x, ones):
    hi = x.astype(BF16)
    rest = x - hi.astype(F32)
    mid = rest.astype(BF16)
    low = (rest - mid.astype(F32)).astype(BF16)
    return dot(hi, ones, NN) + dot(mid, ones, NN) + dot(low, ones, NN)


D_ROW = 0
D_COL = D_ROW + 8
F_ROW = D_COL + 4
F_COL = F_ROW + 8
S_UP = F_COL + 4
S_DOWN = S_UP + 8
T_UP = S_DOWN + 8
T_DOWN = T_UP + 4
Q_STEP = T_DOWN + 4
R_UP = Q_STEP + 10
R_DOWN = R_UP + 8
W_DP = R_DOWN + 8
W_Y = W_DP + 1
W_Z = W_Y + 6
COPIES = W_Z + 8


def kernel(
    q_ref, k_ref, v_ref, cot_ref, ow_ref, decay_ref, gates_ref,
    qg_ref, kg_ref, vg_ref, dg_ref, gg_ref, wg_ref,
    x_ref, xt_ref, zc_ref, zt_ref, flow_ref,
    dbuf, dcol, fbuf, fcol, etab, ctab,
    sbuf, tbuf, qs_ref, qa, qb, qc, qb2, qc2, pbuf, rsend, rrecv,
    g_ref, lifted_ref, lev_ref, attl_ref, qloc, kloc, vloc, att_ref,
    wbuf, wdp, usum, wa1, wb1, wa2, wb2, sa2, sb2, zsum, wz,
    ssem, rsem,
):
    ctx = lax.axis_index("ctx")
    dp = lax.axis_index("dp")
    y = lax.div(ctx, NZ)
    z = lax.rem(ctx, NZ)

    def zz(j):
        return lax.rem(z + j + NZ, NZ)

    def yy(j):
        return lax.rem(y + j + NY, NY)

    def at_z(j):
        return {"ctx": y * NZ + zz(j)}

    def at_y(j):
        return {"ctx": yy(j) * NZ + z}

    other = {"dp": 1 - dp}
    sent = []

    def copy(src, dst, n, where):
        return pltpu.make_async_remote_copy(
            src_ref=src, dst_ref=dst, send_sem=ssem.at[n], recv_sem=rsem.at[n],
            device_id=where, device_id_type=MESH,
        )

    def send(src, dst, n, where):
        c = copy(src, dst, n, where)
        c.start()
        sent.append(c)

    def arrived(dst, n, where):
        copy(dst, dst, n, where).wait_recv()

    barrier = pltpu.get_barrier_semaphore()
    for j in range(1, NZ):
        pl.semaphore_signal(barrier, inc=1, device_id=at_z(j), device_id_type=MESH)
    for j in range(1, NY):
        pl.semaphore_signal(barrier, inc=1, device_id=at_y(j), device_id_type=MESH)
    pl.semaphore_signal(barrier, inc=1, device_id=other, device_id_type=MESH)

    x_ref[...] = jnp.zeros_like(x_ref)
    x_ref[0:16, :] = gates_ref[...]
    x_ref[16:18, :] = decay_ref[...]
    upto = (iota((ROWS, ROWS), 0) <= iota((ROWS, ROWS), 1)).astype(BF16)
    cum = exact_dot(x_ref[16:24, :], upto)
    x_ref[24:32, :] = cum
    xt_ref[...] = jnp.transpose(x_ref[...])
    total = jnp.broadcast_to(cum[:, ROWS - 1 : ROWS], (8, 128))
    dbuf[pl.ds(z, 1)] = total[None]

    def cols(h):
        return slice(h * DH, (h + 1) * DH)

    def cum_col(h):
        return xt_ref[:, 24 + h : 25 + h]

    def to_end(h):
        return jnp.exp(x_ref[24 + h : 25 + h, ROWS - 1 : ROWS] - cum_col(h))

    def lift(h, m):
        return xt_ref[:, h * 8 + 3 + m : h * 8 + 4 + m] * jnp.exp(cum_col(h))

    for h in range(2):
        scaled = (to_end(h) * v_ref[:, cols(h)].astype(F32)).astype(BF16)
        sbuf[pl.ds(z, 1), h] = dot(k_ref[:, cols(h)], scaled, TN)[None]

    pl.semaphore_wait(barrier, NZ - 1 + NY - 1 + 1)

    for j in range(1, NZ):
        send(dbuf.at[z], dbuf.at[z], D_ROW + j, at_z(j))
    for h in range(2):
        send(sbuf.at[z, h], sbuf.at[z, h], S_UP + h, at_z(1))
        send(sbuf.at[z, h], sbuf.at[z, h], S_DOWN + h, at_z(-1))

    mixed = dot(cot_ref[...], ow_ref[...].reshape(256, 1024), NT).astype(BF16)
    ri, ci = iota((ROWS, ROWS), 0), iota((ROWS, ROWS), 1)
    perm = (ri == 2 * (ci & (DH - 1)) + jnp.right_shift(ci, 7)).astype(BF16)
    g_ref[...] = dot(mixed, perm, NN).astype(BF16)

    def make_qs(h):
        g = g_ref[:, cols(h)].astype(F32)
        for m in range(FAR):
            lifted_ref[h, :, m * DH : (m + 1) * DH] = (lift(h, m) * g).astype(BF16)
        allq = dot(q_ref[:, cols(h)], lifted_ref[h], TN)
        for m in range(FAR):
            qs_ref[h, m] = allq[:, m * DH : (m + 1) * DH]

    for h in range(2):
        make_qs(h)
        send(qs_ref.at[h, 4], qc.at[h], Q_STEP + h, at_y(-1))
        send(qs_ref.at[h, 4], qb.at[h], Q_STEP + 2 + h, at_y(1))
        send(qs_ref.at[h, 3], qa.at[h], Q_STEP + 4 + h, at_y(-1))

    for j in range(1, NZ):
        arrived(dbuf.at[zz(-j)], D_ROW + j, at_z(j))
    zero = jnp.zeros((8, 128), F32)
    running = zero
    before = []
    mine = zero
    for i in range(NZ):
        before.append(running)
        d = dbuf[i]
        mine = mine + jnp.where(i < z, d, zero)
        running = running + d
    row_total = running
    for i in range(NZ):
        after = before[i] + dbuf[i]
        etab[i] = jnp.exp(row_total - after)
        low = i < z
        ctab[i] = jnp.where(low, jnp.exp(jnp.where(low, mine - after, zero)), zero)
    dcol[pl.ds(y, 1), 0:8, :] = row_total[None]
    dcol[pl.ds(y, 1), 8:16, :] = mine[None]
    for j in range(1, NY):
        send(dcol.at[y], dcol.at[y], D_COL + j, at_y(j))

    def gather_step(k):
        for h in range(2):
            if k < 3 or h == 0:
                arrived(sbuf.at[zz(-k), h], S_UP + 2 * (k - 1) + h, at_z(1))
                send(sbuf.at[zz(-k), h], sbuf.at[zz(-k), h], S_UP + 2 * k + h, at_z(1))
            if k < 3 or h == 1:
                arrived(sbuf.at[zz(k), h], S_DOWN + 2 * (k - 1) + h, at_z(-1))
                send(sbuf.at[zz(k), h], sbuf.at[zz(k), h], S_DOWN + 2 * k + h, at_z(-1))

    def attend(h):
        q, k, v, g = q_ref[:, cols(h)], k_ref[:, cols(h)], v_ref[:, cols(h)], g_ref[:, cols(h)]
        rows, columns = iota((ROWS, ROWS), 0), iota((ROWS, ROWS), 1)
        causal = rows >= columns
        split = jnp.bitwise_xor(jnp.right_shift(rows, 6), jnp.right_shift(columns, 6))
        gap = cum_col(h) - x_ref[24 + h : 25 + h, :]
        decay = jnp.where(causal, jnp.exp(jnp.where(causal, gap, 0.0)), 0.0)
        gate = [xt_ref[:, h * 8 + l : h * 8 + l + 1] for l in range(3)]
        picked = jnp.where(split == 0, gate[0], jnp.where(split == 1, gate[1], gate[2]))
        mixing = picked * decay
        scores = dot(q, k, NT)
        gw = dot(g, v, NT)
        weights = (mixing * scores).astype(BF16)
        sg = gw * mixing
        sg_low = sg.astype(BF16)
        attl_ref[h] = dot(weights, v, NN)
        vloc[h] = dot(weights, g, TN)
        qloc[h] = dot(sg_low, k, NN)
        kloc[h] = dot(sg_low, q, TN)
        flow_ref[h : h + 1, :] = jnp.sum(sg * scores, 0, keepdims=True)
        plain = gw * scores * decay
        near = jnp.zeros((ROWS, 1), F32)
        for l in range(3):
            hit = (split == l) if l < 2 else (split >= 2)
            part = jnp.sum(jnp.where(hit, plain, 0.0), 1, keepdims=True)
            zc_ref[:, h * 8 + l : h * 8 + l + 1] = part
            near = near + gate[l] * part
        zc_ref[:, 16 + h : 17 + h] = near

    zc_ref[...] = jnp.zeros_like(zc_ref)
    flow_ref[...] = jnp.zeros_like(flow_ref)
    gather_step(1)
    attend(0)
    gather_step(2)
    for h in range(2):
        arrived(qc.at[h], Q_STEP + h, at_y(-1))
        send(qc.at[h], qc2.at[h], Q_STEP + 6 + h, at_y(-1))
        arrived(qb.at[h], Q_STEP + 2 + h, at_y(1))
        send(qb.at[h], qb2.at[h], Q_STEP + 8 + h, at_y(1))
    attend(1)
    gather_step(3)

    for j in range(1, NY):
        arrived(dcol.at[yy(-j)], D_COL + j, at_y(j))
    row1, row2 = dcol[1, 0:8, :], dcol[2, 0:8, :]
    w2, w3 = jnp.exp(dcol[2, 8:16, :]), jnp.exp(dcol[3, 8:16, :])
    wnext = jnp.exp(dcol[yy(1), 8:16, :])
    ca = jnp.where(lax.rem(y, 2) == 0, wnext, zero)
    cb = jnp.where(y == 0, w3 * jnp.exp(row1 + row2), zero)
    cb2 = jnp.where(y == 1, w3 * jnp.exp(row2), zero)
    cc = jnp.where(y == 1, w2, zero)
    cc2 = jnp.where(y == 0, w2 * jnp.exp(row1), zero)
    for h in range(2):
        arrived(qa.at[h], Q_STEP + 4 + h, at_y(-1))
        arrived(qc2.at[h], Q_STEP + 6 + h, at_y(-1))
        arrived(qb2.at[h], Q_STEP + 8 + h, at_y(1))
        s = slice(h, h + 1)
        pbuf[h] = (
            ca[s] * qa[h] + cb[s] * qb[h] + cb2[s] * qb2[h] + cc[s] * qc[h] + cc2[s] * qc2[h]
        )

    def contribution(h, target):
        e = etab[target, h : h + 1, :]
        c = ctab[target, h : h + 1, :]
        none = jnp.zeros_like(c)
        far = lax.div(target, 4) != lax.div(z, 4)
        same = lax.div(target, 2) == lax.div(z, 2)
        c3 = jnp.where(far, c, none)
        c1 = jnp.where(same, c, none)
        c2 = c - c3 - c1
        return e * pbuf[h] + c1 * qs_ref[h, 0] + c2 * qs_ref[h, 1] + c3 * qs_ref[h, 2]

    def reduce_step(k):
        for h in range(2):
            for up in (0, 1):
                first = 0 if h == 1 - up else 1
                if k < first:
                    continue
                sign = 1 if up else -1
                base = R_UP if up else R_DOWN
                mine_part = contribution(h, zz(sign * (4 - k)))
                if k > first:
                    arrived(rrecv.at[up, h, k - 1], base + 2 * (k - 1) + h, at_z(sign))
                    mine_part = mine_part + rrecv[up, h, k - 1]
                rsend[up, h, k] = mine_part
                send(rsend.at[up, h, k], rrecv.at[up, h, k], base + 2 * k + h, at_z(sign))

    reduce_step(0)

    reduce_step(1)

    for h in range(2):
        for k in range(1, 5):
            if k == 4:
                if h == 0:
                    arrived(sbuf.at[zz(-4), h], S_UP + 6 + h, at_z(1))
                else:
                    arrived(sbuf.at[zz(4), h], S_DOWN + 6 + h, at_z(-1))
                continue
            if k == 3:
                if h == 1:
                    arrived(sbuf.at[zz(-3), h], S_UP + 4 + h, at_z(1))
                else:
                    arrived(sbuf.at[zz(3), h], S_DOWN + 4 + h, at_z(-1))
        lev = [jnp.zeros((DH, DH), F32) for _ in range(3)]
        whole = jnp.zeros((DH, DH), F32)
        for i in range(NZ):
            s = sbuf[i, h]
            c = ctab[i, h : h + 1, :]
            none = jnp.zeros_like(c)
            far = lax.div(z, 4) != i // 4
            same = lax.div(z, 2) == i // 2
            c3 = jnp.where(far, c, none)
            c1 = jnp.where(same, c, none)
            c2 = c - c3 - c1
            lev[0] = lev[0] + c1 * s
            lev[1] = lev[1] + c2 * s
            lev[2] = lev[2] + c3 * s
            whole = whole + etab[i, h : h + 1, :] * s
        for m in range(3):
            lev_ref[h, :, m * DH : (m + 1) * DH] = lev[m].astype(BF16)
        tbuf[pl.ds(y, 1), h] = whole[None]
        send(tbuf.at[y, h], tbuf.at[y, h], T_UP + h, at_y(1))
        send(tbuf.at[y, h], tbuf.at[y, h], T_DOWN + h, at_y(-1))

    reduce_step(2)
    arrived(tbuf.at[yy(-1), 0], T_UP + 0, at_y(1))
    send(tbuf.at[yy(-1), 0], tbuf.at[yy(-1), 0], T_UP + 2, at_y(1))
    arrived(tbuf.at[yy(1), 1], T_DOWN + 1, at_y(-1))
    send(tbuf.at[yy(1), 1], tbuf.at[yy(1), 1], T_DOWN + 2, at_y(-1))
    arrived(tbuf.at[yy(-1), 1], T_UP + 1, at_y(1))
    arrived(tbuf.at[yy(1), 0], T_DOWN + 0, at_y(-1))
    reduce_step(3)
    arrived(tbuf.at[yy(-2), 0], T_UP + 2, at_y(1))
    arrived(tbuf.at[yy(2), 1], T_DOWN + 2, at_y(-1))

    f4 = jnp.where(lax.rem(y, 2) == 1, jnp.exp(mine), zero)
    f5 = jnp.where(y >= 2, jnp.exp(mine + jnp.where(y == 3, row2, zero)), zero)
    f5low = f5 * jnp.exp(row1)

    def far_rows(h):
        s = slice(h, h + 1)
        lev_ref[h, :, 3 * DH : 4 * DH] = (f4[s] * tbuf[yy(-1), h]).astype(BF16)
        lev_ref[h, :, 4 * DH : 5 * DH] = (f5[s] * tbuf[1, h] + f5low[s] * tbuf[0, h]).astype(BF16)
        projected = dot(q_ref[:, cols(h)], lev_ref[h], NN)
        g = g_ref[:, cols(h)].astype(F32)
        attended = attl_ref[h]
        extra = zc_ref[:, 16 + h : 17 + h]
        ecum = jnp.exp(cum_col(h))
        for m in range(FAR):
            part = projected[:, m * DH : (m + 1) * DH]
            coef = lift(h, m)
            attended = attended + coef * part
            inner = jnp.sum(part * g, 1, keepdims=True)
            zc_ref[:, h * 8 + 3 + m : h * 8 + 4 + m] = ecum * inner
            extra = extra + coef * inner
        zc_ref[:, 16 + h : 17 + h] = extra
        att_ref[:, cols(h)] = attended.astype(BF16)

    for h in range(2):
        far_rows(h)

    r, j = iota((512, ROWS), 0), iota((512, ROWS), 1)
    wanted = (r & 1) * DH + jnp.right_shift(r, 3) * 2 + (jnp.right_shift(r, 1) & 1)
    half = jnp.right_shift(r, 2) & 1
    match = wanted == j
    first_half = jnp.where(match & (half == 0), 1.0, 0.0).astype(BF16)
    second_half = jnp.where(match & (half == 1), 1.0, 0.0).astype(BF16)
    att = att_ref[...]
    lhs0 = dot(first_half, att, NT).astype(BF16)
    lhs1 = dot(second_half, att, NT).astype(BF16)
    wbuf[...] = dot(lhs0, cot_ref[:, 0:512], NN) + dot(lhs1, cot_ref[:, 512:1024], NN)
    theirs = pl.multiple_of((1 - dp) * 256, 256)
    ours = pl.multiple_of(dp * 256, 256)
    send(wbuf.at[pl.ds(theirs, 256)], wdp, W_DP, other)

    for h in range(2):
        qfar = dot(lifted_ref[h], lev_ref[h], NT)
        qg_ref[:, cols(h)] = (qloc[h] + qfar).astype(BF16)

    arrived(wdp, W_DP, other)
    usum[...] = wbuf[pl.ds(ours, 256), :] + wdp[...]

    def chunk(jy, start):
        return pl.ds(pl.multiple_of(yy(jy) * 64 + start, 32), 32)

    send(usum.at[chunk(2, 0)], wa1, W_Y + 0, at_y(1))
    send(usum.at[chunk(-2, 32)], wb1, W_Y + 1, at_y(-1))
    send(usum.at[chunk(1, 32)], wa2.at[pl.ds(32, 32)], W_Y + 2, at_y(1))
    send(usum.at[chunk(-1, 0)], wb2.at[pl.ds(0, 32)], W_Y + 3, at_y(-1))

    zt_ref[...] = jnp.transpose(zc_ref[...])
    gg_ref[...] = zt_ref[0:16, :]
    for h in range(2):
        arrived(rrecv.at[1, h, 3], R_UP + 6 + h, at_z(1))
        arrived(rrecv.at[0, h, 3], R_DOWN + 6 + h, at_z(-1))
        e = etab[z, h : h + 1, :]
        returned = (e * pbuf[h] + rrecv[1, h, 3] + rrecv[0, h, 3]).astype(BF16)
        k, v = k_ref[:, cols(h)], v_ref[:, cols(h)]
        w = to_end(h)
        kfar = w * dot(v, returned, NT)
        vfar = w * dot(k, returned, NN)
        kg_ref[:, cols(h)] = (kloc[h] + kfar).astype(BF16)
        vg_ref[:, cols(h)] = (vloc[h] + vfar).astype(BF16)
        zc_ref[:, 24 + h : 25 + h] = jnp.sum(k.astype(F32) * kfar, 1, keepdims=True)

    arrived(wa1, W_Y + 0, at_y(1))
    sa2[...] = usum[chunk(1, 0), :] + wa1[...]
    send(sa2, wa2.at[pl.ds(0, 32)], W_Y + 4, at_y(1))
    arrived(wb1, W_Y + 1, at_y(-1))
    sb2[...] = usum[chunk(-1, 32), :] + wb1[...]
    send(sb2, wb2.at[pl.ds(32, 32)], W_Y + 5, at_y(-1))

    back = jnp.transpose(zc_ref[...])
    flow = zt_ref[16:24, :] - flow_ref[...] - back[24:32, :]
    block_flow = jnp.broadcast_to(jnp.sum(flow, 1, keepdims=True), (8, 128))
    fbuf[pl.ds(z, 1)] = block_flow[None]
    for jz in range(1, NZ):
        send(fbuf.at[z], fbuf.at[z], F_ROW + jz, at_z(jz))
    onward = (iota((ROWS, ROWS), 0) >= iota((ROWS, ROWS), 1)).astype(BF16)
    within = exact_dot(flow, onward)

    arrived(wa2.at[pl.ds(32, 32)], W_Y + 2, at_y(1))
    arrived(wb2.at[pl.ds(0, 32)], W_Y + 3, at_y(-1))
    arrived(wa2.at[pl.ds(0, 32)], W_Y + 4, at_y(1))
    arrived(wb2.at[pl.ds(32, 32)], W_Y + 5, at_y(-1))
    own = pl.ds(pl.multiple_of(y * 64, 64), 64)
    zsum[...] = usum[own, :] + wa2[...] + wb2[...]

    def part_of(jz):
        return pl.ds(pl.multiple_of(zz(jz) * 8, 8), 8)

    for jz in (4, 3, 5, 2, 6, 1, 7):
        send(zsum.at[part_of(jz)], wz.at[jz], W_Z + jz, at_z(jz))

    tail = zero
    row_flow = zero
    for jz in range(1, NZ):
        arrived(fbuf.at[zz(-jz)], F_ROW + jz, at_z(jz))
    for i in range(NZ):
        f = fbuf[i]
        row_flow = row_flow + f
        tail = tail + jnp.where(i > z, f, zero)
    fcol[pl.ds(y, 1)] = row_flow[None]
    for jy in range(1, NY):
        send(fcol.at[y], fcol.at[y], F_COL + jy, at_y(jy))

    result = zsum[part_of(0), :]
    for jz in range(1, NZ):
        arrived(wz.at[jz], W_Z + jz, at_z(jz))
        result = result + wz[jz]
    for i in range(2):
        wg_ref[i, :, 0:512] = result[2 * i : 2 * i + 2, :]
        wg_ref[i, :, 512:1024] = result[4 + 2 * i : 6 + 2 * i, :]

    for jy in range(1, NY):
        arrived(fcol.at[yy(-jy)], F_COL + jy, at_y(jy))
    for i in range(NY):
        tail = tail + jnp.where(i > y, fcol[i], zero)
    dg_ref[...] = (within + tail[:, 0:1])[0:2, :]

    for c in sent:
        c.wait_send()


def hand_over(*refs):
    for i in range(6):
        refs[6 + i][...] = refs[i][...]


def local(queries, key_vectors, value_vectors, out_cotangent, out_weight, log_decay, level_gates):
    v32 = lambda *s: pltpu.VMEM(s, F32)
    v16 = lambda *s: pltpu.VMEM(s, BF16)
    vmem = pl.BlockSpec(memory_space=pltpu.VMEM)
    scratch = [
        v32(128, ROWS), v32(ROWS, 128), v32(ROWS, 128), v32(128, ROWS), v32(8, ROWS),
        v32(NZ, 8, 128), v32(NY, 16, 128), v32(NZ, 8, 128), v32(NY, 8, 128),
        v32(NZ, 8, 128), v32(NZ, 8, 128),
        v32(NZ, 2, DH, DH), v32(NY, 2, DH, DH), v32(2, FAR, DH, DH),
        v32(2, DH, DH), v32(2, DH, DH), v32(2, DH, DH), v32(2, DH, DH), v32(2, DH, DH),
        v32(2, DH, DH), v32(2, 2, 4, DH, DH), v32(2, 2, 4, DH, DH),
        v16(ROWS, 256), v16(2, ROWS, FAR * DH), v16(2, DH, FAR * DH), v32(2, ROWS, DH),
        v32(2, ROWS, DH), v32(2, ROWS, DH), v32(2, ROWS, DH), v16(ROWS, 256),
        v32(512, 512), v32(256, 512), v32(256, 512), v32(32, 512), v32(32, 512),
        v32(64, 512), v32(64, 512), v32(32, 512), v32(32, 512), v32(64, 512), v32(NZ, 8, 512),
        pltpu.SemaphoreType.DMA((COPIES,)), pltpu.SemaphoreType.DMA((COPIES,)),
    ]
    outs = pl.pallas_call(
        kernel,
        out_shape=(
            jax.ShapeDtypeStruct((ROWS, 256), BF16),
            jax.ShapeDtypeStruct((ROWS, 256), BF16),
            jax.ShapeDtypeStruct((ROWS, 256), BF16),
            jax.ShapeDtypeStruct((2, ROWS), F32),
            jax.ShapeDtypeStruct((16, ROWS), F32),
            jax.ShapeDtypeStruct((2, 2, 1024), F32),
        ),
        in_specs=[vmem] * 7,
        out_specs=(vmem,) * 6,
        scratch_shapes=scratch,
        compiler_params=pltpu.CompilerParams(collective_id=0, has_side_effects=True),
    )(
        queries[0], key_vectors[0], value_vectors[0], out_cotangent[0],
        out_weight, log_decay[0], level_gates[0].reshape(16, ROWS),
    )
    qg, kg, vg, dg, gg, wg = pl.pallas_call(
        hand_over,
        out_shape=tuple(jax.ShapeDtypeStruct(o.shape, o.dtype) for o in outs),
        in_specs=[vmem] * 6,
        out_specs=(vmem,) * 6,
    )(*outs)
    return (
        qg[None], kg[None], vg[None], dg[None],
        gg.reshape(1, 2, 8, ROWS), wg,
    )


def solution(mesh):
    placed = (
        P("dp", "ctx", "head"),
        P("dp", "ctx", "head"),
        P("dp", "ctx", "head"),
        P("dp", "ctx", None),
        P(None, "head", None),
        P("dp", "head", "ctx"),
        P("dp", "head", None, "ctx"),
    )
    return jax.shard_map(
        local,
        mesh=mesh,
        in_specs=placed,
        out_specs=(
            P("dp", "ctx", "head"),
            P("dp", "ctx", "head"),
            P("dp", "ctx", "head"),
            P("dp", "head", "ctx"),
            P("dp", "head", None, "ctx"),
            P(("dp", "ctx"), "head", None),
        ),
        check_vma=False,
    )
```
